128 devices in a mesh: pb: 8 (over z, core), ka: 16 (over x, y).
Axes of the slice: x: 4, y: 4, z: 4, core: 2. Of those that a mesh axis runs over, the one named last changes fastest.
Arguments:
- queries: bfloat16 [16384, 2048], P('pb'), may hold values from -8 to 8
- keys: bfloat16 [16384, 2048], P(('ka', 'pb')), may hold values from -8 to 8
- values: bfloat16 [16384, 2048], P(('ka', 'pb')), may hold values from -6 to 6
- block_mask: int32 [128, 128], P('pb', 'ka'), may hold values from 0 to 1, as said below
Outputs:
- attended: bfloat16 [16384, 2048], P('pb')
The draws below stay inside these ranges and needn't reach their ends.
Inputs may be any that keep to these rules, and one draw needn't show every extreme that they name: `block_mask`: 1 where the two blocks are equal or adjacent, in the first 2 block rows and block columns, and for 3 block columns drawn for each block row; 0 elsewhere.
All inputs are finite; a program needn't handle non-finite values.
Results may differ from the reference program's by a relative error of at most 0.0047.
Values may be sent and summed in bfloat16 or wider, within the bound.
A program may use at most 128 MiB of HBM per device.

```python
import jax
import jax.numpy as jnp
from jax import lax

HEADS = 16
HEAD_DIM = 128
BLOCK = 128
GLOBAL = 2
RANDOM = 3
D = 2048
TOKENS = 16384
NB = 128


def paired_rows(key):
    base_q = jax.random.normal(jax.random.fold_in(key, 1), (TOKENS, D), jnp.float32)
    base_k = jax.random.normal(jax.random.fold_in(key, 2), (TOKENS, D), jnp.float32)
    return (jnp.clip(base_q, -8.0, 8.0), jnp.clip(base_k, -8.0, 8.0))


def draw_queries(key, part):
    return paired_rows(key)[0].astype(jnp.bfloat16)


def draw_keys(key, part):
    return paired_rows(key)[1].astype(jnp.bfloat16)


def draw_block_mask(key, part):
    row_ids = jnp.arange(NB, dtype=jnp.int32)[:, None]
    col_ids = jnp.arange(NB, dtype=jnp.int32)[None, :]
    near = jnp.abs(row_ids - col_ids) <= 1
    global_part = (row_ids < GLOBAL) | (col_ids < GLOBAL)
    picks = jax.random.randint(jax.random.fold_in(key, 9), (NB, RANDOM), 0, NB)
    random_part = jnp.any(picks[:, :, None] == col_ids[:, None, :], axis=1)
    return (near | global_part | random_part).astype(jnp.int32)


def block_scale(key, extent, cuts, smallest, high):
    def one(dim, blocks):
        draws = jax.random.uniform(jax.random.fold_in(jax.random.fold_in(key, 6), dim), (blocks,), jnp.float32, smallest / len(cuts), high / len(cuts))
        return jnp.repeat(jnp.exp(draws), extent[dim] // blocks).reshape((-1,) + (1,) * (len(extent) - dim - 1))

    loudness = one(*cuts[0])
    for cut in cuts[1:]:
        loudness = loudness * one(*cut)
    return loudness


def bell_draw(rng, extent, width, bound, cuts=(), kind=jnp.bfloat16):
    loudness = block_scale(rng, extent, cuts, -0.22, 0.18) if cuts else 1.0
    entries = jax.random.normal(rng, extent, jnp.float32) * width * loudness
    return jnp.minimum(jnp.maximum(entries, -bound), bound).astype(kind)


def setup_inputs(seed: int = 0) -> dict:
    key_of = jax.random.split(jax.random.key(seed), 5)
    queries = draw_queries(jax.random.fold_in(key_of[4], 71), 0)
    keys = draw_keys(jax.random.fold_in(key_of[4], 71), 0)
    values = bell_draw(key_of[2], (TOKENS, D), 1.0, 6.0, ((0, 128),))
    block_mask = draw_block_mask(jax.random.fold_in(key_of[4], 71), 0)
    return {"queries": queries, "keys": keys, "values": values, "block_mask": block_mask}


NEG = -1e30


def reference(queries, keys, values, block_mask):
    scale = HEAD_DIM ** -0.5
    nblocks = TOKENS // BLOCK

    def one_head(head_index):
        start = (head_index * HEAD_DIM).astype(jnp.int32)
        q_head = lax.dynamic_slice_in_dim(queries, start, HEAD_DIM, 1)
        k_head = lax.dynamic_slice_in_dim(keys, start, HEAD_DIM, 1)
        v_head = lax.dynamic_slice_in_dim(values, start, HEAD_DIM, 1)
        q_blocks = q_head.reshape(nblocks, BLOCK, HEAD_DIM)

        def one_block(pair):
            q_rows, mask_row = pair
            allowed = jnp.repeat(mask_row, BLOCK) > 0
            scores = jnp.dot(q_rows, k_head.T, preferred_element_type=jnp.float32) * scale
            row_top = jnp.max(jnp.where(allowed[None, :], scores, NEG), axis=1, keepdims=True)
            weights = jnp.where(allowed[None, :], jnp.exp(scores - row_top), 0.0)
            totals = jnp.sum(weights, axis=1, keepdims=True)
            numer = jnp.dot(weights.astype(jnp.bfloat16), v_head, preferred_element_type=jnp.float32)
            return (numer / totals).astype(jnp.bfloat16)

        return lax.map(one_block, (q_blocks, block_mask))

    stacked = lax.map(one_head, jnp.arange(HEADS).astype(jnp.int32))
    return stacked.transpose(1, 2, 0, 3).reshape(TOKENS, HEADS * HEAD_DIM)
```

```python
import functools

import jax
import jax.numpy as jnp
from jax import lax
from jax.experimental import pallas as pl
from jax.experimental.pallas import tpu as pltpu
from jax.sharding import PartitionSpec as P

HEADS = 16
HEAD_DIM = 128
BLOCK = 128
NPB = 8
NKA = 16
ROWS = 2048
QBLOCKS = ROWS // BLOCK
SLOTS = 8
MESH = pl.DeviceIdType.MESH
BF16 = jnp.bfloat16
F32 = jnp.float32
SCALE = HEAD_DIM ** (-0.5) * 1.4426950408889634
NEG = -1e30


def remote(src, dst, send, recv, pb, ka):
    return pltpu.make_async_remote_copy(
        src_ref=src,
        dst_ref=dst,
        send_sem=send,
        recv_sem=recv,
        device_id={"pb": pb, "ka": ka},
        device_id_type=MESH,
    )


def greet(peers):
    barrier = pltpu.get_barrier_semaphore()
    for pb, ka in peers:
        pl.semaphore_signal(
            barrier, inc=1, device_id={"pb": pb, "ka": ka}, device_id_type=MESH
        )
    pl.semaphore_wait(barrier, len(peers))


def gather_kernel(
    k_ref, v_ref, m_ref, kb_ref, vb_ref, mb_ref,
    own_sem, a_send, a_recv, m_send, m_recv, z_send, z_recv,
):
    pb = lax.axis_index("pb")
    ka = lax.axis_index("ka")
    other = pb + 1 - 2 * (pb % 2)
    up = (pb + 2) % NPB
    down = (pb + 6) % NPB
    far = (pb + 4) % NPB

    def peer_of(d):
        hi, lo = ka // 4, ka % 4

        def xor2(a, b):
            if b == 0:
                return a
            if b == 1:
                return a + 1 - 2 * (a % 2)
            if b == 2:
                return (a + 2) % 4
            return 3 - a

        return xor2(hi, d // 4) * 4 + xor2(lo, d % 4)

    peers = [peer_of(d) for d in range(NKA)]
    greet(
        [(pb, peers[d]) for d in range(1, NKA)] + [(other, ka), (up, ka), (down, ka)]
    )

    def cols(i):
        return pl.ds(pl.multiple_of(i * HEAD_DIM, HEAD_DIM), HEAD_DIM)

    srcs, bufs = (k_ref, v_ref), (kb_ref, vb_ref)
    owns = []
    for t in range(2):
        c = pltpu.make_async_copy(srcs[t].at[:, cols(ka)], bufs[t].at[pb, ka], own_sem.at[t])
        c.start()
        owns.append(c)
    own_m = pltpu.make_async_copy(m_ref, mb_ref.at[ka], own_sem.at[2])
    own_m.start()
    sends = []
    for t in range(2):
        for d in range(1, NKA):
            c = remote(
                srcs[t].at[:, cols(peers[d])], bufs[t].at[pb, ka],
                a_send.at[t, d], a_recv.at[t, d], pb, peers[d],
            )
            c.start()
            sends.append(c)
    for d in range(1, NKA):
        c = remote(m_ref, mb_ref.at[ka], m_send.at[d], m_recv.at[d], pb, peers[d])
        c.start()
        sends.append(c)

    def group(buf, who, g, first=0, count=4):
        base = (peers[4 * g] // 4) * 4 + first
        return buf.at[who, pl.ds(base, count)]

    def send(kind, step, ref, to):
        c = remote(ref, ref, z_send.at[kind, step], z_recv.at[kind, step], to, ka)
        c.start()
        sends.append(c)

    def arrived(kind, step, ref):
        remote(ref, ref, z_send.at[kind, step], z_recv.at[kind, step], up, ka).wait_recv()

    for step in range(10):
        if step < 8:
            t, g = divmod(step, 4)
            if g == 0:
                owns[t].wait()
            for d in range(4 * g, 4 * g + 4):
                if d:
                    ref = bufs[t].at[pb, peers[d]]
                    remote(ref, ref, a_send.at[t, d], a_recv.at[t, d], pb, ka).wait_recv()
            mine = group(bufs[t], pb, g)
            send(0, step, mine, up)
            send(1, step, mine, down)
            send(2, step, mine, other)
        if 1 <= step < 9:
            t, g = divmod(step - 1, 4)
            low = group(bufs[t], down, g)
            arrived(0, step - 1, low)
            send(3, step - 1, group(bufs[t], down, g, 0, 2), up)
            send(5, step - 1, low, other)
            high = group(bufs[t], up, g)
            arrived(1, step - 1, high)
            send(4, step - 1, group(bufs[t], up, g, 2, 2), down)
            send(6, step - 1, high, other)
        if 2 <= step:
            t, g = divmod(step - 2, 4)
            a = group(bufs[t], far, g, 0, 2)
            arrived(3, step - 2, a)
            send(7, step - 2, a, other)
            b = group(bufs[t], far, g, 2, 2)
            arrived(4, step - 2, b)
            send(8, step - 2, b, other)
    ob = other
    for step in range(8):
        t, g = divmod(step, 4)
        arrived(2, step, group(bufs[t], ob, g))
        arrived(5, step, group(bufs[t], (ob + 6) % NPB, g))
        arrived(6, step, group(bufs[t], (ob + 2) % NPB, g))
        arrived(7, step, group(bufs[t], (ob + 4) % NPB, g, 0, 2))
        arrived(8, step, group(bufs[t], (ob + 4) % NPB, g, 2, 2))
    own_m.wait()
    for d in range(1, NKA):
        ref = mb_ref.at[peers[d]]
        remote(ref, ref, m_send.at[d], m_recv.at[d], pb, ka).wait_recv()
    for c in sends:
        c.wait_send()


def gather(keys, values, mask_t):
    shape = jax.ShapeDtypeStruct((NPB, NKA, BLOCK, HEAD_DIM), BF16)
    any_spec = pl.BlockSpec(memory_space=pl.ANY)
    dma = pltpu.SemaphoreType.DMA
    return pl.pallas_call(
        gather_kernel,
        out_shape=(shape, shape, jax.ShapeDtypeStruct((NKA, 8, 128), jnp.int32)),
        in_specs=[any_spec] * 3,
        out_specs=(any_spec,) * 3,
        scratch_shapes=[
            dma((3,)), dma((2, NKA)), dma((2, NKA)), dma((NKA,)), dma((NKA,)),
            dma((9, 8)), dma((9, 8)),
        ],
        compiler_params=pltpu.CompilerParams(collective_id=0, has_side_effects=True),
        name="gather",
    )(keys, values, mask_t)


def attend_kernel(
    q_hbm, k_hbm, v_hbm, m_ref, o_hbm,
    q_ref, k_ref, v_ref, o_ref, tab_v, tab_s, acc, top, tot, sems,
):
    pb = lax.axis_index("pb")
    ka = lax.axis_index("ka")
    qc = pltpu.make_async_copy(
        q_hbm.at[:, pl.ds(pl.multiple_of(ka * HEAD_DIM, HEAD_DIM), HEAD_DIM)], q_ref, sems.at[0]
    )
    kc = pltpu.make_async_copy(k_hbm, k_ref, sems.at[1])
    vc = pltpu.make_async_copy(v_hbm, v_ref, sems.at[2])
    qc.start()
    kc.start()
    vc.start()

    live = (m_ref[...].reshape(NKA * 8, 128) > 0).astype(F32)
    row = lax.broadcasted_iota(jnp.int32, (128, 128), 0)
    col = lax.broadcasted_iota(jnp.int32, (128, 128), 1)
    lower = (col <= row).astype(F32)
    rank = jnp.dot(lower.astype(BF16), live.astype(BF16), preferred_element_type=F32)
    weight = live * row.astype(F32)
    parts = [
        jnp.sum(jnp.where(rank == s + 1, weight, 0.0), axis=0, keepdims=True)
        for s in range(SLOTS)
    ]
    count = jnp.sum(live, axis=0, keepdims=True)
    table = jnp.concatenate(parts + [jnp.broadcast_to(count, (8, 128))], axis=0)
    tab_v[...] = table.astype(jnp.int32)
    tc = pltpu.make_async_copy(tab_v, tab_s, sems.at[3])
    tc.start()
    tc.wait()
    qc.wait()
    kc.wait()
    vc.wait()

    first = jnp.where(pb == 0, 2, 0)

    def scores(q, k):
        return lax.dot_general(q, k, (((1,), (1,)), ((), ())), preferred_element_type=F32)

    def block(i, carry):
        rows = pl.ds(pl.multiple_of(i * BLOCK, BLOCK), BLOCK)
        q = q_ref[rows, :]
        n = tab_s[SLOTS, i]
        js = [tab_s[s, i] for s in range(SLOTS)]
        ss = []
        for s in range(SLOTS):
            k = k_ref[js[s] % NPB, js[s] // NPB]
            ss.append(scores(q, k) * SCALE + jnp.where(s < n, 0.0, NEG))
        m = ss[0]
        for s in range(1, SLOTS):
            m = jnp.maximum(m, ss[s])
        m = jnp.max(m, axis=1, keepdims=True)
        total = None
        out = None
        for s in range(SLOTS):
            p = jnp.exp2(ss[s] - m)
            total = p if total is None else total + p
            v = v_ref[js[s] % NPB, js[s] // NPB]
            o = jnp.dot(p.astype(BF16), v, preferred_element_type=F32)
            out = o if out is None else out + o
        out = out / jnp.sum(total, axis=1, keepdims=True)
        o_ref[rows, :] = out.astype(BF16)
        return carry

    lax.fori_loop(first, QBLOCKS, block, 0)

    @pl.when(pb == 0)
    def _():
        q = q_ref[0 : 2 * BLOCK, :]
        acc[...] = jnp.zeros_like(acc)
        tot[...] = jnp.zeros_like(tot)
        top[...] = jnp.full_like(top, NEG)

        def chunk(c, carry):
            b, half = c // 2, c % 2
            k = k_ref[b, pl.ds(half * 8, 8)].reshape(8 * BLOCK, HEAD_DIM)
            v = v_ref[b, pl.ds(half * 8, 8)].reshape(8 * BLOCK, HEAD_DIM)
            s = scores(q, k) * SCALE
            old = top[...]
            m = jnp.maximum(old, jnp.max(s, axis=1, keepdims=True))
            p = jnp.exp2(s - m[:, :1])
            a = jnp.exp2(old - m)
            tot[...] = a * tot[...] + jnp.sum(p, axis=1, keepdims=True)
            acc[...] = a * acc[...] + jnp.dot(p.astype(BF16), v, preferred_element_type=F32)
            top[...] = m
            return carry

        lax.fori_loop(0, 16, chunk, 0)
        o_ref[0 : 2 * BLOCK, :] = (acc[...] / tot[...]).astype(BF16)

    oc = pltpu.make_async_copy(o_ref, o_hbm.at[ka], sems.at[4])
    oc.start()
    oc.wait()


def attend(queries, kbuf, vbuf, mbuf):
    any_spec = pl.BlockSpec(memory_space=pl.ANY)
    shape = (NPB, NKA, BLOCK, HEAD_DIM)
    return pl.pallas_call(
        attend_kernel,
        out_shape=jax.ShapeDtypeStruct((NKA, ROWS, HEAD_DIM), BF16),
        in_specs=[any_spec] * 3 + [pl.BlockSpec(memory_space=pltpu.VMEM)],
        out_specs=any_spec,
        scratch_shapes=[
            pltpu.VMEM((ROWS, HEAD_DIM), BF16),
            pltpu.VMEM(shape, BF16),
            pltpu.VMEM(shape, BF16),
            pltpu.VMEM((ROWS, HEAD_DIM), BF16),
            pltpu.VMEM((16, 128), jnp.int32),
            pltpu.SMEM((16, 128), jnp.int32),
            pltpu.VMEM((2 * BLOCK, HEAD_DIM), F32),
            pltpu.VMEM((2 * BLOCK, HEAD_DIM), F32),
            pltpu.VMEM((2 * BLOCK, HEAD_DIM), F32),
            pltpu.SemaphoreType.DMA((5,)),
        ],
        name="attend",
    )(queries, kbuf, vbuf, mbuf)


HALF = ROWS // 2
PIECE = ROWS // 4


def spread_kernel(in_ref, out_ref, send_sem, recv_sem):
    del in_ref
    pb = lax.axis_index("pb")
    ka = lax.axis_index("ka")
    x, y = ka // 4, ka % 4

    def at(dx, dy):
        return ((x + dx + 4) % 4) * 4 + (y + dy + 4) % 4

    greet([(pb, at(1, 0)), (pb, at(3, 0)), (pb, at(0, 1)), (pb, at(0, 3))])
    sends = []

    def place(a, u, w):
        return at(u, w) if a == 0 else at(w, u)

    def ref(a, u, w, piece):
        lo, n = (0, 2) if piece is None else (piece, 1)
        return out_ref.at[place(a, u, w), pl.ds(a * HALF + lo * PIECE, n * PIECE)]

    def sem_id(u, w, piece):
        return ((u % 4) * 4 + w % 4) * 3 + (2 if piece is None else piece)

    def send(a, u, w, piece, du, dw):
        i = sem_id(u - du, w - dw, piece)
        r = ref(a, u, w, piece)
        c = remote(r, r, send_sem.at[a, i], recv_sem.at[a, i], pb, place(a, du, dw))
        c.start()
        sends.append(c)

    def arrived(a, u, w, piece):
        i = sem_id(u, w, piece)
        r = ref(a, u, w, piece)
        remote(r, r, send_sem.at[a, i], recv_sem.at[a, i], pb, ka).wait_recv()

    both = (0, 1)
    for a in both:
        send(a, 0, 0, None, 1, 0)
        send(a, 0, 0, None, -1, 0)
    for a in both:
        send(a, 0, 0, None, 0, 1)
        send(a, 0, 0, None, 0, -1)
    for a in both:
        arrived(a, -1, 0, None)
        send(a, -1, 0, 0, 1, 0)
        arrived(a, 1, 0, None)
        send(a, 1, 0, 1, -1, 0)
    for a in both:
        for u in (-1, 1):
            send(a, u, 0, None, 0, 1)
            send(a, u, 0, None, 0, -1)
    for a in both:
        arrived(a, 0, -1, None)
        send(a, 0, -1, 0, 0, 1)
        arrived(a, 0, 1, None)
        send(a, 0, 1, 1, 0, -1)
    for a in both:
        for piece in (0, 1):
            arrived(a, 2, 0, piece)
            send(a, 2, 0, piece, 0, 1)
            send(a, 2, 0, piece, 0, -1)
    for u in (-1, 1):
        for a in both:
            arrived(a, u, -1, None)
            send(a, u, -1, 0, 0, 1)
            arrived(a, u, 1, None)
            send(a, u, 1, 1, 0, -1)
    for a in both:
        arrived(a, 2, -1, 0)
        send(a, 2, -1, 0, 0, 1)
        arrived(a, 2, 1, 0)
    for a in both:
        arrived(a, 2, 1, 1)
        send(a, 2, 1, 1, 0, -1)
        arrived(a, 2, -1, 1)
    for a in both:
        for u in (0, -1, 1, 2):
            for piece in (0, 1):
                arrived(a, u, 2, piece)
    for c in sends:
        c.wait_send()


def spread(mine):
    any_spec = pl.BlockSpec(memory_space=pl.ANY)
    return pl.pallas_call(
        spread_kernel,
        out_shape=jax.ShapeDtypeStruct((NKA, ROWS, HEAD_DIM), BF16),
        in_specs=[any_spec],
        out_specs=any_spec,
        input_output_aliases={0: 0},
        scratch_shapes=[pltpu.SemaphoreType.DMA((2, 48)), pltpu.SemaphoreType.DMA((2, 48))],
        compiler_params=pltpu.CompilerParams(collective_id=1, has_side_effects=True),
        name="spread",
    )(mine)


def weave_kernel(in_ref, out_ref):
    out_ref[...] = in_ref[0]


def weave(heads):
    return pl.pallas_call(
        weave_kernel,
        out_shape=jax.ShapeDtypeStruct((ROWS, HEADS * HEAD_DIM), BF16),
        grid=(HEADS,),
        in_specs=[pl.BlockSpec((1, ROWS, HEAD_DIM), lambda h: (h, 0, 0))],
        out_specs=pl.BlockSpec((ROWS, HEAD_DIM), lambda h: (0, h)),
        name="weave",
    )(heads)


def local(queries, keys, values, block_mask):
    mask_t = jnp.pad(block_mask.T, ((0, 0), (0, 112)))
    kbuf, vbuf, mbuf = gather(keys, values, mask_t)
    mine = attend(queries, kbuf, vbuf, mbuf)
    return weave(spread(mine))


def solution(mesh):
    return jax.shard_map(
        local,
        mesh=mesh,
        in_specs=(P("pb", None), P(("ka", "pb"), None), P(("ka", "pb"), None), P("pb", "ka")),
        out_specs=P("pb", None),
        check_vma=False,
    )
```

```python
import jax
import jax.numpy as jnp
from jax import lax
from jax.experimental import pallas as pl
from jax.experimental.pallas import tpu as pltpu
from jax.sharding import PartitionSpec as P

HEADS = 16
HEAD_DIM = 128
BLOCK = 128
NB = 128
NPB = 8
NKA = 16
ROWS = 2048
QBLOCKS = ROWS // BLOCK
SLOTS = 8
WAVE = HEAD_DIM // 2
PACKED = ROWS // 2
HALF = PACKED // 2
PIECE = PACKED // 4
DENSE = 2 * BLOCK
MESH = pl.DeviceIdType.MESH
BF16 = jnp.bfloat16
F32 = jnp.float32
SCALE = HEAD_DIM ** (-0.5) * 1.4426950408889634
NEG = -1e30


def remote(src, dst, send, recv, pb, ka):
    return pltpu.make_async_remote_copy(
        src_ref=src,
        dst_ref=dst,
        send_sem=send,
        recv_sem=recv,
        device_id={"pb": pb, "ka": ka},
        device_id_type=MESH,
    )


def greet(peers):
    barrier = pltpu.get_barrier_semaphore()
    for pb, ka in peers:
        pl.semaphore_signal(
            barrier, inc=1, device_id={"pb": pb, "ka": ka}, device_id_type=MESH
        )
    pl.semaphore_wait(barrier, len(peers))


def xor2(a, b):
    if b == 0:
        return a
    if b == 1:
        return a + 1 - 2 * (a % 2)
    if b == 2:
        return (a + 2) % 4
    return 3 - a


def nt(a, b):
    return lax.dot_general(a, b, (((1,), (1,)), ((), ())), preferred_element_type=F32)


def attend_kernel(
    q_hbm, k_hbm, v_hbm, m_hbm, out_ref,
    got, q_ref, v_own, vt_own, kb, vb0, vb1, mb, tab_v, tab_s, p_ref, tot_ref,
    sg, pg, mg, gtot, gacc,
    own_sem, a_send, a_recv, m_send, m_recv, z_send, z_recv, s_send, s_recv,
):
    pb = lax.axis_index("pb")
    ka = lax.axis_index("ka")
    other = pb + 1 - 2 * (pb % 2)
    up, down, far = (pb + 2) % NPB, (pb + 6) % NPB, (pb + 4) % NPB
    x, y = ka // 4, ka % 4
    vbs = (vb0, vb1)
    sends = []

    def cols(i):
        return pl.ds(pl.multiple_of(i * HEAD_DIM, HEAD_DIM), HEAD_DIM)

    vc = pltpu.make_async_copy(v_hbm, v_own, own_sem.at[0])
    vc.start()
    qc = pltpu.make_async_copy(q_hbm.at[:, cols(ka)], q_ref, own_sem.at[1])
    qc.start()
    kc = pltpu.make_async_copy(k_hbm.at[:, cols(ka)], kb.at[pb * NKA + ka], own_sem.at[2])
    kc.start()
    mc = pltpu.make_async_copy(m_hbm, mb.at[ka], own_sem.at[3])
    mc.start()

    peers = [xor2(x, d // 4) * 4 + xor2(y, d % 4) for d in range(NKA)]
    greet(
        [(pb, peers[d]) for d in range(1, NKA)] + [(other, ka), (up, ka), (down, ka)]
    )

    def begin(c):
        c.start()
        sends.append(c)

    for d in range(1, NKA):
        begin(remote(
            k_hbm.at[:, cols(peers[d])], kb.at[pb * NKA + ka],
            a_send.at[0, d], a_recv.at[0, d], pb, peers[d],
        ))
    for d in range(1, NKA):
        begin(remote(m_hbm, mb.at[ka], m_send.at[d], m_recv.at[d], pb, peers[d]))
    own_v = []

    def turn_values():
        vc.wait()
        for h in range(HEADS):
            tile = v_own[:, h * HEAD_DIM : (h + 1) * HEAD_DIM]
            vt_own[h * HEAD_DIM : (h + 1) * HEAD_DIM, :] = tile.T
        for w in range(2):
            def half(p, w=w):
                return pl.ds(pl.multiple_of(p * HEAD_DIM + w * WAVE, WAVE), WAVE)

            c = pltpu.make_async_copy(vt_own.at[half(ka)], vbs[w].at[pb * NKA + ka], own_sem.at[4 + w])
            c.start()
            own_v.append(c)
            for d in range(1, NKA):
                begin(remote(
                    vt_own.at[half(peers[d])], vbs[w].at[pb * NKA + ka],
                    a_send.at[1 + w, d], a_recv.at[1 + w, d], pb, peers[d],
                ))

    bufs = (kb, vb0, vb1)

    def group(buf, who, g, first=0, count=4):
        return buf.at[pl.ds(who * NKA + xor2(x, g) * 4 + first, count)]

    def send(kind, item, ref, to):
        begin(remote(ref, ref, z_send.at[kind, item], z_recv.at[kind, item], to, ka))

    def arrived(kind, item, ref):
        remote(ref, ref, z_send.at[kind, item], z_recv.at[kind, item], up, ka).wait_recv()

    def own(t):
        n, g = divmod(t, 4)
        if g == 0:
            (kc if n == 0 else own_v[n - 1]).wait()
        for d in range(4 * g, 4 * g + 4):
            if d:
                ref = bufs[n].at[pb * NKA + peers[d]]
                remote(ref, ref, a_send.at[n, d], a_recv.at[n, d], pb, ka).wait_recv()
        mine = group(bufs[n], pb, g)
        send(0, t, mine, up)
        send(1, t, mine, down)
        send(2, t, mine, other)

    def near(t):
        n, g = divmod(t, 4)
        low = group(bufs[n], down, g)
        arrived(0, t, low)
        send(3, t, group(bufs[n], down, g, 0, 2), up)
        send(5, t, low, other)
        high = group(bufs[n], up, g)
        arrived(1, t, high)
        send(4, t, group(bufs[n], up, g, 2, 2), down)
        send(6, t, high, other)

    def distant(t):
        n, g = divmod(t, 4)
        a = group(bufs[n], far, g, 0, 2)
        arrived(3, t, a)
        send(7, t, a, other)
        b = group(bufs[n], far, g, 2, 2)
        arrived(4, t, b)
        send(8, t, b, other)

    def relayed(t):
        n, g = divmod(t, 4)
        arrived(2, t, group(bufs[n], other, g))
        arrived(5, t, group(bufs[n], (other + 6) % NPB, g))
        arrived(6, t, group(bufs[n], (other + 2) % NPB, g))
        arrived(7, t, group(bufs[n], (other + 4) % NPB, g, 0, 2))
        arrived(8, t, group(bufs[n], (other + 4) % NPB, g, 2, 2))

    def make_table():
        mc.wait()
        for d in range(1, NKA):
            ref = mb.at[peers[d]]
            remote(ref, ref, m_send.at[d], m_recv.at[d], pb, ka).wait_recv()
        live = (mb[...].reshape(NB, 128) > 0).astype(F32)
        row = lax.broadcasted_iota(jnp.int32, (NB, 128), 0)
        col = lax.broadcasted_iota(jnp.int32, (NB, 128), 1)
        lower = (col <= row).astype(F32).astype(BF16)
        rank = jnp.dot(lower, live.astype(BF16), preferred_element_type=F32)
        weight = live * ((row % NPB) * NKA + row // NPB).astype(F32)
        parts = [
            jnp.sum(jnp.where(rank == s + 1, weight, 0.0), axis=0, keepdims=True)
            for s in range(SLOTS)
        ]
        count = jnp.sum(live, axis=0, keepdims=True)
        table = jnp.concatenate(parts + [jnp.broadcast_to(count, (8, 128))], axis=0)
        tab_v[...] = table.astype(jnp.int32)
        tc = pltpu.make_async_copy(tab_v, tab_s, own_sem.at[6])
        tc.start()
        tc.wait()

    def place(s, i):
        return jnp.minimum(jnp.maximum(tab_s[s, i], 0), NB - 1)

    def weigh(i, carry):
        q = q_ref[pl.ds(pl.multiple_of(i * BLOCK, BLOCK), BLOCK), :]
        n = tab_s[SLOTS, i]
        ss = []
        for s in range(SLOTS):
            k = kb[place(s, i)]
            ss.append(nt(q, k) * SCALE + jnp.where(s < n, 0.0, NEG))
        m = ss[0]
        for s in range(1, SLOTS):
            m = jnp.maximum(m, ss[s])
        m = jnp.max(m, axis=1, keepdims=True)
        total = None
        for s in range(SLOTS):
            p = jnp.exp2(ss[s] - m)
            total = p if total is None else total + p
            p_ref[i, s] = p.astype(BF16)
        tot_ref[i] = jnp.broadcast_to(jnp.sum(total, axis=1, keepdims=True), (BLOCK, 128))
        return carry

    def gathered(w, i):
        out = None
        for s in range(SLOTS):
            o = nt(p_ref[i, s], vbs[w][place(s, i)])
            out = o if out is None else out + o
        return out / tot_ref[i, :, :WAVE]

    def value(w):
        def pair(i, carry):
            o = jnp.concatenate([gathered(w, i), gathered(w, i + 8)], axis=1)
            got[w, ka, pl.ds(pl.multiple_of(i * BLOCK, BLOCK), BLOCK), :] = o.astype(BF16)
            return carry

        lax.fori_loop(0, QBLOCKS // 2, pair, 0)

        @pl.when(pb == 0)
        def _():
            dense = (gacc[w] / gtot[...])[:, :WAVE].astype(BF16)
            right = got[w, ka, 0:DENSE, WAVE:]
            got[w, ka, 0:DENSE, :] = jnp.concatenate([dense, right], axis=1)

    def dense_weigh(g):
        @pl.when(pb == 0)
        def _():
            q = q_ref[0:DENSE, :]
            base = xor2(x, g) * 4

            def score(b, m):
                k = kb[pl.ds(b * NKA + base, 4)].reshape(4 * BLOCK, HEAD_DIM)
                s = nt(q, k) * SCALE
                sg[b] = s
                for j in range(4):
                    m = jnp.maximum(m, s[:, j * 128 : (j + 1) * 128])
                return m

            old = mg[g - 1] if g else jnp.full((DENSE, 128), NEG, F32)
            m = lax.fori_loop(0, NPB, score, old)
            m = jnp.broadcast_to(jnp.max(m, axis=1, keepdims=True), (DENSE, 128))
            mg[g] = m

            def expo(b, total):
                for j in range(4):
                    p = jnp.exp2(sg[b, :, j * 128 : (j + 1) * 128] - mg[g])
                    total = total + p
                    pg[g, b, :, j * 128 : (j + 1) * 128] = p.astype(BF16)
                return total

            total = lax.fori_loop(0, NPB, expo, jnp.zeros((DENSE, 128), F32))
            total = jnp.broadcast_to(jnp.sum(total, axis=1, keepdims=True), (DENSE, 128))
            gtot[...] = total + gtot[...] * jnp.exp2(old - m) if g else total

    def dense_value(w, g):
        @pl.when(pb == 0)
        def _():
            base = xor2(x, g) * 4

            def part(b, acc):
                v = vbs[w][pl.ds(b * NKA + base, 4)]
                v = jnp.concatenate([v[j] for j in range(4)], axis=1)
                return acc + nt(pg[g, b], v)

            acc = lax.fori_loop(0, NPB, part, jnp.zeros((DENSE, WAVE), F32))
            acc = acc * jnp.exp2(mg[g] - mg[3])[:, :WAVE]
            acc = jnp.concatenate([acc, acc], axis=1)
            gacc[w] = gacc[w] + acc if g else acc

    def at(dx, dy):
        return ((x + dx + 4) % 4) * 4 + (y + dy + 4) % 4

    class Spread:
        def __init__(self, wave):
            self.wave = wave

        def place(self, a, u, w):
            return at(u, w) if a == 0 else at(w, u)

        def ref(self, a, u, w, piece):
            lo, n = (0, 2) if piece is None else (piece, 1)
            return got.at[
                self.wave, self.place(a, u, w), pl.ds(a * HALF + lo * PIECE, n * PIECE)
            ]

        def sem_id(self, u, w, piece):
            return ((u % 4) * 4 + w % 4) * 3 + (2 if piece is None else piece)

        def send(self, a, u, w, piece, du, dw):
            i = self.sem_id(u - du, w - dw, piece)
            r = self.ref(a, u, w, piece)
            begin(remote(
                r, r, s_send.at[self.wave, a, i], s_recv.at[self.wave, a, i],
                pb, self.place(a, du, dw),
            ))

        def arrived(self, a, u, w, piece):
            i = self.sem_id(u, w, piece)
            r = self.ref(a, u, w, piece)
            remote(
                r, r, s_send.at[self.wave, a, i], s_recv.at[self.wave, a, i], pb, ka
            ).wait_recv()

        def stage(self, n):
            send, arrived = self.send, self.arrived
            both = (0, 1)
            if n == 0:
                for a in both:
                    send(a, 0, 0, None, 1, 0)
                    send(a, 0, 0, None, -1, 0)
                for a in both:
                    send(a, 0, 0, None, 0, 1)
                    send(a, 0, 0, None, 0, -1)
            elif n == 1:
                for a in both:
                    arrived(a, -1, 0, None)
                    send(a, -1, 0, 0, 1, 0)
                    arrived(a, 1, 0, None)
                    send(a, 1, 0, 1, -1, 0)
                for a in both:
                    for u in (-1, 1):
                        send(a, u, 0, None, 0, 1)
                        send(a, u, 0, None, 0, -1)
            elif n == 2:
                for a in both:
                    arrived(a, 0, -1, None)
                    send(a, 0, -1, 0, 0, 1)
                    arrived(a, 0, 1, None)
                    send(a, 0, 1, 1, 0, -1)
            elif n == 3:
                for a in both:
                    for piece in (0, 1):
                        arrived(a, 2, 0, piece)
                        send(a, 2, 0, piece, 0, 1)
                        send(a, 2, 0, piece, 0, -1)
            elif n == 4:
                for u in (-1, 1):
                    for a in both:
                        arrived(a, u, -1, None)
                        send(a, u, -1, 0, 0, 1)
                        arrived(a, u, 1, None)
                        send(a, u, 1, 1, 0, -1)
            elif n == 5:
                for a in both:
                    arrived(a, 2, -1, 0)
                    send(a, 2, -1, 0, 0, 1)
                    arrived(a, 2, 1, 0)
                for a in both:
                    arrived(a, 2, 1, 1)
                    send(a, 2, 1, 1, 0, -1)
                    arrived(a, 2, -1, 1)
            else:
                for a in both:
                    for u in (0, -1, 1, 2):
                        for piece in (0, 1):
                            arrived(a, u, 2, piece)

    def unpack(a, u, w, piece):
        h = first.place(a, u, w)
        lo, n = (0, 2) if piece is None else (piece, 1)
        lanes = pl.ds(pl.multiple_of(h * HEAD_DIM, HEAD_DIM), HEAD_DIM)

        def rows(r, carry):
            at_row = a * HALF + lo * PIECE + r * BLOCK
            src = pl.ds(pl.multiple_of(at_row, BLOCK), BLOCK)
            low, high = got[0, h, src, :], got[1, h, src, :]
            out_ref[src, lanes] = jnp.concatenate([low[:, :WAVE], high[:, :WAVE]], axis=1)
            dst = pl.ds(pl.multiple_of(PACKED + at_row, BLOCK), BLOCK)
            out_ref[dst, lanes] = jnp.concatenate([low[:, WAVE:], high[:, WAVE:]], axis=1)
            return carry

        lax.fori_loop(0, n * PIECE // BLOCK, rows, 0)

    both = (0, 1)
    first, second = Spread(0), Spread(1)
    own(0)
    own(1)
    turn_values()
    own(2)
    near(0)
    qc.wait()
    make_table()
    own(3)
    for t in range(4):
        near(t + 1)
        distant(t)
        relayed(t)
        if t < 3:
            own(t + 4)
        dense_weigh(t)
    lax.fori_loop(0, 3, weigh, 0)
    own(7)
    near(5)
    distant(4)
    relayed(4)
    dense_value(0, 0)
    lax.fori_loop(3, 6, weigh, 0)
    near(6)
    distant(5)
    relayed(5)
    dense_value(0, 1)
    lax.fori_loop(6, 9, weigh, 0)
    near(7)
    own(8)
    distant(6)
    relayed(6)
    dense_value(0, 2)
    lax.fori_loop(9, 12, weigh, 0)
    distant(7)
    own(9)
    lax.fori_loop(12, 16, weigh, 0)
    relayed(7)
    dense_value(0, 3)
    value(0)
    first.stage(0)
    near(8)
    own(10)
    near(9)
    distant(8)
    relayed(8)
    dense_value(1, 0)
    own(11)
    first.stage(1)
    near(10)
    distant(9)
    relayed(9)
    dense_value(1, 1)
    near(11)
    distant(10)
    relayed(10)
    dense_value(1, 2)
    first.stage(2)
    distant(11)
    relayed(11)
    dense_value(1, 3)
    value(1)
    second.stage(0)
    for a in both:
        unpack(a, 0, 0, None)
    first.stage(3)
    first.stage(4)
    second.stage(1)
    for a in both:
        unpack(a, -1, 0, None)
        unpack(a, 1, 0, None)
    first.stage(5)
    second.stage(2)
    for a in both:
        unpack(a, 0, -1, None)
        unpack(a, 0, 1, None)
    first.stage(6)
    second.stage(3)
    for a in both:
        unpack(a, 2, 0, None)
    second.stage(4)
    for a in both:
        for u in (-1, 1):
            unpack(a, u, -1, None)
            unpack(a, u, 1, None)
    second.stage(5)
    for a in both:
        unpack(a, 2, -1, None)
        unpack(a, 2, 1, None)
    for u in (0, -1, 1, 2):
        for a in both:
            for piece in (0, 1):
                second.arrived(a, u, 2, piece)
                unpack(a, u, 2, piece)
    for c in sends:
        c.wait_send()


def attend(queries, keys, values, mask_t):
    any_spec = pl.BlockSpec(memory_space=pltpu.HBM)
    dma = pltpu.SemaphoreType.DMA
    vmem = pltpu.VMEM
    return pl.pallas_call(
        attend_kernel,
        out_shape=pltpu.VMEM((ROWS, HEADS * HEAD_DIM), BF16),
        in_specs=[any_spec] * 4,
        out_specs=pl.BlockSpec(memory_space=pltpu.VMEM),
        scratch_shapes=[
            vmem((2, NKA, PACKED, 128), BF16),
            vmem((ROWS, HEAD_DIM), BF16),
            vmem((BLOCK, HEADS * HEAD_DIM), BF16),
            vmem((HEADS * HEAD_DIM, BLOCK), BF16),
            vmem((NB, BLOCK, HEAD_DIM), BF16),
            vmem((NB, WAVE, BLOCK), BF16),
            vmem((NB, WAVE, BLOCK), BF16),
            vmem((NKA, 8, 128), jnp.int32),
            vmem((16, 128), jnp.int32),
            pltpu.SMEM((16, 128), jnp.int32),
            vmem((QBLOCKS, SLOTS, BLOCK, BLOCK), BF16),
            vmem((QBLOCKS, BLOCK, 128), F32),
            vmem((NPB, DENSE, 4 * BLOCK), F32),
            vmem((4, NPB, DENSE, 4 * BLOCK), BF16),
            vmem((4, DENSE, 128), F32),
            vmem((DENSE, 128), F32),
            vmem((2, DENSE, 128), F32),
            dma((7,)), dma((3, NKA)), dma((3, NKA)), dma((NKA,)), dma((NKA,)),
            dma((9, 12)), dma((9, 12)), dma((2, 2, 48)), dma((2, 2, 48)),
        ],
        compiler_params=pltpu.CompilerParams(
            collective_id=0, has_side_effects=True, vmem_limit_bytes=58_400_000
        ),
        name="attend",
    )(queries, keys, values, mask_t)


def local(queries, keys, values, block_mask):
    mask_t = jnp.pad(block_mask.T, ((0, 0), (0, 112)))
    return attend(queries, keys, values, mask_t)


def solution(mesh):
    return jax.shard_map(
        local,
        mesh=mesh,
        in_specs=(P("pb", None), P(("ka", "pb"), None), P(("ka", "pb"), None), P("pb", "ka")),
        out_specs=P("pb", None),
        check_vma=False,
    )
```

```python
import jax
import jax.numpy as jnp
from jax import lax
from jax.experimental import pallas as pl
from jax.experimental.pallas import tpu as pltpu
from jax.sharding import PartitionSpec as P

HEADS = 16
HEAD_DIM = 128
BLOCK = 128
NB = 128
NPB = 8
NKA = 16
ROWS = 2048
QBLOCKS = ROWS // BLOCK
SLOTS = 8
WAVE = HEAD_DIM // 2
PACKED = ROWS // 2
HALF = PACKED // 2
PIECE = PACKED // 4
DENSE = 2 * BLOCK
MESH = pl.DeviceIdType.MESH
BF16 = jnp.bfloat16
F32 = jnp.float32
SCALE = HEAD_DIM ** (-0.5) * 1.4426950408889634
NEG = -1e30


def remote(src, dst, send, recv, pb, ka):
    return pltpu.make_async_remote_copy(
        src_ref=src,
        dst_ref=dst,
        send_sem=send,
        recv_sem=recv,
        device_id={"pb": pb, "ka": ka},
        device_id_type=MESH,
    )


def greet(peers):
    barrier = pltpu.get_barrier_semaphore()
    for pb, ka in peers:
        pl.semaphore_signal(
            barrier, inc=1, device_id={"pb": pb, "ka": ka}, device_id_type=MESH
        )
    pl.semaphore_wait(barrier, len(peers))


def xor2(a, b):
    if b == 0:
        return a
    if b == 1:
        return a + 1 - 2 * (a % 2)
    if b == 2:
        return (a + 2) % 4
    return 3 - a


def nt(a, b):
    return lax.dot_general(a, b, (((1,), (1,)), ((), ())), preferred_element_type=F32)


def attend_kernel(
    q_hbm, k_hbm, v_hbm, m_hbm, out_ref,
    got, q_ref, v_own, vt_own, kb, vb0, vb1, mb, tab_v, tab_s, p_ref, tot_ref,
    sg, pg, mg, gtot, gacc,
    sem, a_recv, z_send, z_recv, s_send, s_recv,
):
    pb = lax.axis_index("pb")
    ka = lax.axis_index("ka")
    other = pb + 1 - 2 * (pb % 2)
    up, down, far = (pb + 2) % NPB, (pb + 6) % NPB, (pb + 4) % NPB
    x, y = ka // 4, ka % 4
    vbs = (vb0, vb1)

    def cols(i):
        return pl.ds(pl.multiple_of(i * HEAD_DIM, HEAD_DIM), HEAD_DIM)

    vc = pltpu.make_async_copy(v_hbm, v_own, sem.at[0])
    vc.start()
    qc = pltpu.make_async_copy(q_hbm.at[:, cols(ka)], q_ref, sem.at[1])
    pltpu.make_async_copy(k_hbm.at[:, cols(ka)], kb.at[pb * NKA + ka], a_recv.at[0]).start()
    pltpu.make_async_copy(m_hbm, mb.at[ka], sem.at[3]).start()

    peers = [xor2(x, d // 4) * 4 + xor2(y, d % 4) for d in range(NKA)]
    greet(
        [(pb, peers[d]) for d in range(1, NKA)] + [(other, ka), (up, ka), (down, ka)]
    )

    def take(s, ref):
        remote(ref, ref, s, s, pb, ka).wait_recv()

    def half(p, w):
        return pl.ds(pl.multiple_of(p * HEAD_DIM + w * WAVE, WAVE), WAVE)

    def exchange(n, g):
        for d in range(4 * g, 4 * g + 4):
            if d:
                src = vt_own.at[half(peers[d], n - 1)] if n else k_hbm.at[:, cols(peers[d])]
                dst = (kb, vb0, vb1)[n].at[pb * NKA + ka]
                remote(src, dst, sem.at[5 + n], a_recv.at[n * 4 + g], pb, peers[d]).start()

    def turn_values():
        vc.wait()
        for h in range(HEADS):
            tile = v_own[:, h * HEAD_DIM : (h + 1) * HEAD_DIM]
            vt_own[h * HEAD_DIM : (h + 1) * HEAD_DIM, :] = tile.T
        for w in range(2):
            pltpu.make_async_copy(
                vt_own.at[half(ka, w)], vbs[w].at[pb * NKA + ka], a_recv.at[4 + 4 * w]
            ).start()

    exchange(0, 0)
    exchange(0, 1)
    for d in range(1, NKA):
        remote(m_hbm, mb.at[ka], sem.at[4], sem.at[3], pb, peers[d]).start()
    qc.start()

    bufs = (kb, vb0, vb1)

    def group(buf, who, g, first=0, count=4):
        return buf.at[pl.ds(who * NKA + xor2(x, g) * 4 + first, count)]

    NEAR, DISTANT, RELAYED = 0, 12, 24

    def send(t, kind, ref, to):
        remote(ref, ref, z_send.at[t // 4], z_recv.at[kind + t], to, ka).start()

    def own(t):
        n, g = divmod(t, 4)
        mine = group(bufs[n], pb, g)
        take(a_recv.at[t], mine)
        send(t, NEAR, mine, up)
        send(t, NEAR, mine, down)
        send(t, RELAYED, mine, other)

    def near(t):
        n, g = divmod(t, 4)
        take(z_recv.at[NEAR + t], bufs[n].at[pl.ds(0, 8)])
        send(t, DISTANT, group(bufs[n], down, g, 0, 2), up)
        send(t, DISTANT, group(bufs[n], up, g, 2, 2), down)
        send(t, RELAYED, group(bufs[n], down, g), other)
        send(t, RELAYED, group(bufs[n], up, g), other)

    def distant(t):
        n, g = divmod(t, 4)
        both = group(bufs[n], far, g)
        take(z_recv.at[DISTANT + t], both)
        send(t, RELAYED, both, other)

    def relayed(t):
        take(z_recv.at[RELAYED + t], bufs[t // 4].at[pl.ds(0, 16)])

    def make_table():
        take(sem.at[3], mb)
        live = (mb[...].reshape(NB, 128) > 0).astype(F32)
        row = lax.broadcasted_iota(jnp.int32, (NB, 128), 0)
        col = lax.broadcasted_iota(jnp.int32, (NB, 128), 1)
        lower = (col <= row).astype(F32).astype(BF16)
        rank = jnp.dot(lower, live.astype(BF16), preferred_element_type=F32)
        weight = live * ((row % NPB) * NKA + row // NPB).astype(F32)
        parts = [
            jnp.sum(jnp.where(rank == s + 1, weight, 0.0), axis=0, keepdims=True)
            for s in range(SLOTS)
        ]
        count = jnp.sum(live, axis=0, keepdims=True)
        table = jnp.concatenate(parts + [jnp.broadcast_to(count, (8, 128))], axis=0)
        tab_v[...] = table.astype(jnp.int32)
        tc = pltpu.make_async_copy(tab_v, tab_s, sem.at[2])
        tc.start()
        tc.wait()

    def place(s, i):
        return jnp.minimum(jnp.maximum(tab_s[s, i], 0), NB - 1)

    def weigh(i, carry):
        q = q_ref[pl.ds(pl.multiple_of(i * BLOCK, BLOCK), BLOCK), :]
        n = tab_s[SLOTS, i]
        ss = []
        for s in range(SLOTS):
            k = kb[place(s, i)]
            ss.append(nt(q, k) * SCALE + jnp.where(s < n, 0.0, NEG))
        m = ss[0]
        for s in range(1, SLOTS):
            m = jnp.maximum(m, ss[s])
        m = jnp.max(m, axis=1, keepdims=True)
        total = None
        for s in range(SLOTS):
            p = jnp.exp2(ss[s] - m)
            total = p if total is None else total + p
            p_ref[i, s] = p.astype(BF16)
        tot_ref[i] = jnp.broadcast_to(jnp.sum(total, axis=1, keepdims=True), (BLOCK, 128))
        return carry

    def gathered(w, i):
        out = None
        for s in range(SLOTS):
            o = nt(p_ref[i, s], vbs[w][place(s, i)])
            out = o if out is None else out + o
        return out / tot_ref[i, :, :WAVE]

    def value(w):
        def pair(i, carry):
            o = jnp.concatenate([gathered(w, i), gathered(w, i + 8)], axis=1)
            got[w, ka, pl.ds(pl.multiple_of(i * BLOCK, BLOCK), BLOCK), :] = o.astype(BF16)
            return carry

        lax.fori_loop(0, QBLOCKS // 2, pair, 0)

        @pl.when(pb == 0)
        def _():
            dense = (gacc[w] / gtot[...])[:, :WAVE].astype(BF16)
            right = got[w, ka, 0:DENSE, WAVE:]
            got[w, ka, 0:DENSE, :] = jnp.concatenate([dense, right], axis=1)

    def dense_weigh(g):
        @pl.when(pb == 0)
        def _():
            q = q_ref[0:DENSE, :]
            base = xor2(x, g) * 4

            def score(b, m):
                k = kb[pl.ds(b * NKA + base, 4)].reshape(4 * BLOCK, HEAD_DIM)
                s = nt(q, k) * SCALE
                sg[b] = s
                for j in range(4):
                    m = jnp.maximum(m, s[:, j * 128 : (j + 1) * 128])
                return m

            old = mg[g - 1] if g else jnp.full((DENSE, 128), NEG, F32)
            m = lax.fori_loop(0, NPB, score, old)
            m = jnp.broadcast_to(jnp.max(m, axis=1, keepdims=True), (DENSE, 128))
            mg[g] = m

            def expo(b, total):
                for j in range(4):
                    p = jnp.exp2(sg[b, :, j * 128 : (j + 1) * 128] - mg[g])
                    total = total + p
                    pg[g, b, :, j * 128 : (j + 1) * 128] = p.astype(BF16)
                return total

            total = lax.fori_loop(0, NPB, expo, jnp.zeros((DENSE, 128), F32))
            total = jnp.broadcast_to(jnp.sum(total, axis=1, keepdims=True), (DENSE, 128))
            gtot[...] = total + gtot[...] * jnp.exp2(old - m) if g else total

    def dense_value(w, g):
        @pl.when(pb == 0)
        def _():
            base = xor2(x, g) * 4

            def part(b, acc):
                v = vbs[w][pl.ds(b * NKA + base, 4)]
                v = jnp.concatenate([v[j] for j in range(4)], axis=1)
                return acc + nt(pg[g, b], v)

            acc = lax.fori_loop(0, NPB, part, jnp.zeros((DENSE, WAVE), F32))
            acc = acc * jnp.exp2(mg[g] - mg[3])[:, :WAVE]
            acc = jnp.concatenate([acc, acc], axis=1)
            gacc[w] = gacc[w] + acc if g else acc

    def at(dx, dy):
        return ((x + dx + 4) % 4) * 4 + (y + dy + 4) % 4

    class Spread:
        def __init__(self, wave):
            self.wave = wave

        def place(self, a, u, w):
            return at(u, w) if a == 0 else at(w, u)

        def ref(self, a, u, w, piece):
            lo, n = (0, 2) if piece is None else (piece, 1)
            return got.at[
                self.wave, self.place(a, u, w), pl.ds(a * HALF + lo * PIECE, n * PIECE)
            ]

        def place_id(self, u, w):
            u, w = u % 4, w % 4
            if w == 2:
                return 6 + u
            if w == 0:
                return 2 if u == 2 else 0
            return {0: 1, 3: 3, 1: 4, 2: 5}[u]

        def send(self, a, u, w, piece, du, dw):
            r = self.ref(a, u, w, piece)
            i = self.place_id(u - du, w - dw)
            remote(
                r, r, s_send.at[self.wave], s_recv.at[self.wave, i],
                pb, self.place(a, du, dw),
            ).start()

        def arrived(self, u, w):
            i = self.place_id(u, w)
            heads = {0: 2, 1: 2, 2: 1, 3: 2, 4: 2, 5: 2}.get(i, 1)
            take(s_recv.at[self.wave, i], got.at[self.wave, pl.ds(0, heads)])

        def stage(self, n):
            send, arrived = self.send, self.arrived
            both = (0, 1)
            if n == 0:
                for a in both:
                    send(a, 0, 0, None, 1, 0)
                    send(a, 0, 0, None, -1, 0)
                for a in both:
                    send(a, 0, 0, None, 0, 1)
                    send(a, 0, 0, None, 0, -1)
            elif n == 1:
                arrived(1, 0)
                for a in both:
                    send(a, -1, 0, 0, 1, 0)
                    send(a, 1, 0, 1, -1, 0)
                for a in both:
                    for u in (-1, 1):
                        send(a, u, 0, None, 0, 1)
                        send(a, u, 0, None, 0, -1)
            elif n == 2:
                arrived(0, 1)
                for a in both:
                    send(a, 0, -1, 0, 0, 1)
                    send(a, 0, 1, 1, 0, -1)
            elif n == 3:
                arrived(2, 0)
                for a in both:
                    for piece in (0, 1):
                        send(a, 2, 0, piece, 0, 1)
                        send(a, 2, 0, piece, 0, -1)
            elif n == 4:
                for u in (-1, 1):
                    arrived(u, 1)
                    for a in both:
                        send(a, u, -1, 0, 0, 1)
                        send(a, u, 1, 1, 0, -1)
            elif n == 5:
                arrived(2, 1)
                for a in both:
                    send(a, 2, -1, 0, 0, 1)
                    send(a, 2, 1, 1, 0, -1)
            else:
                for u in (0, -1, 1, 2):
                    arrived(u, 2)

    def unpack(a, u, w, piece):
        h = first.place(a, u, w)
        lo, n = (0, 2) if piece is None else (piece, 1)
        lanes = pl.ds(pl.multiple_of(h * HEAD_DIM, HEAD_DIM), HEAD_DIM)

        def rows(r, carry):
            at_row = a * HALF + lo * PIECE + r * BLOCK
            src = pl.ds(pl.multiple_of(at_row, BLOCK), BLOCK)
            low, high = got[0, h, src, :], got[1, h, src, :]
            out_ref[src, lanes] = jnp.concatenate([low[:, :WAVE], high[:, :WAVE]], axis=1)
            dst = pl.ds(pl.multiple_of(PACKED + at_row, BLOCK), BLOCK)
            out_ref[dst, lanes] = jnp.concatenate([low[:, WAVE:], high[:, WAVE:]], axis=1)
            return carry

        lax.fori_loop(0, n * PIECE // BLOCK, rows, 0)

    both = (0, 1)
    first, second = Spread(0), Spread(1)
    own(0)
    exchange(0, 2)
    own(1)
    exchange(0, 3)
    turn_values()
    near(0)
    own(2)
    exchange(1, 0)
    exchange(1, 1)
    near(1)
    own(3)
    exchange(1, 2)
    exchange(1, 3)
    distant(0)
    relayed(0)
    qc.wait()
    dense_weigh(0)
    near(2)
    distant(1)
    for g in range(4):
        exchange(2, g)
    own(4)
    make_table()
    relayed(1)
    near(3)
    own(5)
    dense_weigh(1)
    distant(2)
    relayed(2)
    near(4)
    own(6)
    dense_weigh(2)
    distant(3)
    relayed(3)
    dense_weigh(3)
    lax.fori_loop(0, 3, weigh, 0)
    own(7)
    near(5)
    distant(4)
    relayed(4)
    dense_value(0, 0)
    lax.fori_loop(3, 6, weigh, 0)
    near(6)
    distant(5)
    relayed(5)
    dense_value(0, 1)
    lax.fori_loop(6, 9, weigh, 0)
    near(7)
    own(8)
    distant(6)
    relayed(6)
    dense_value(0, 2)
    lax.fori_loop(9, 12, weigh, 0)
    distant(7)
    own(9)
    lax.fori_loop(12, 16, weigh, 0)
    relayed(7)
    dense_value(0, 3)
    value(0)
    first.stage(0)
    near(8)
    own(10)
    near(9)
    distant(8)
    relayed(8)
    dense_value(1, 0)
    own(11)
    first.stage(1)
    near(10)
    distant(9)
    relayed(9)
    dense_value(1, 1)
    near(11)
    distant(10)
    relayed(10)
    dense_value(1, 2)
    first.stage(2)
    distant(11)
    relayed(11)
    dense_value(1, 3)
    value(1)
    second.stage(0)
    for a in both:
        unpack(a, 0, 0, None)
    first.stage(3)
    first.stage(4)
    second.stage(1)
    for a in both:
        unpack(a, -1, 0, None)
        unpack(a, 1, 0, None)
    first.stage(5)
    second.stage(2)
    for a in both:
        unpack(a, 0, -1, None)
        unpack(a, 0, 1, None)
    first.stage(6)
    second.stage(3)
    for a in both:
        unpack(a, 2, 0, None)
    second.stage(4)
    for a in both:
        for u in (-1, 1):
            unpack(a, u, -1, None)
            unpack(a, u, 1, None)
    second.stage(5)
    for a in both:
        unpack(a, 2, -1, None)
        unpack(a, 2, 1, None)
    for u in (0, -1, 1, 2):
        second.arrived(u, 2)
        for a in both:
            unpack(a, u, 2, None)
    for s, ref in (
        (sem.at[4], mb.at[pl.ds(0, NKA - 1)]),
        (sem.at[5], kb.at[pl.ds(0, NKA - 1)]),
        (sem.at[6], vb0.at[pl.ds(0, NKA - 1)]),
        (sem.at[7], vb1.at[pl.ds(0, NKA - 1)]),
        (z_send.at[0], kb.at[pl.ds(0, 112)]),
        (z_send.at[1], vb0.at[pl.ds(0, 112)]),
        (z_send.at[2], vb1.at[pl.ds(0, 112)]),
        (s_send.at[0], got.at[0, pl.ds(0, NKA - 1)]),
        (s_send.at[1], got.at[1, pl.ds(0, NKA - 1)]),
    ):
        remote(ref, ref, s, s, pb, ka).wait_send()


def attend(queries, keys, values, mask_t):
    any_spec = pl.BlockSpec(memory_space=pltpu.HBM)
    dma = pltpu.SemaphoreType.DMA
    vmem = pltpu.VMEM
    return pl.pallas_call(
        attend_kernel,
        out_shape=pltpu.VMEM((ROWS, HEADS * HEAD_DIM), BF16),
        in_specs=[any_spec] * 4,
        out_specs=pl.BlockSpec(memory_space=pltpu.VMEM),
        scratch_shapes=[
            vmem((2, NKA, PACKED, 128), BF16),
            vmem((ROWS, HEAD_DIM), BF16),
            vmem((BLOCK, HEADS * HEAD_DIM), BF16),
            vmem((HEADS * HEAD_DIM, BLOCK), BF16),
            vmem((NB, BLOCK, HEAD_DIM), BF16),
            vmem((NB, WAVE, BLOCK), BF16),
            vmem((NB, WAVE, BLOCK), BF16),
            vmem((NKA, 8, 128), jnp.int32),
            vmem((16, 128), jnp.int32),
            pltpu.SMEM((16, 128), jnp.int32),
            vmem((QBLOCKS, SLOTS, BLOCK, BLOCK), BF16),
            vmem((QBLOCKS, BLOCK, 128), F32),
            vmem((NPB, DENSE, 4 * BLOCK), F32),
            vmem((4, NPB, DENSE, 4 * BLOCK), BF16),
            vmem((4, DENSE, 128), F32),
            vmem((DENSE, 128), F32),
            vmem((2, DENSE, 128), F32),
            dma((8,)), dma((12,)), dma((3,)), dma((36,)), dma((2,)), dma((2, 10)),
        ],
        compiler_params=pltpu.CompilerParams(
            collective_id=0, has_side_effects=True, vmem_limit_bytes=58_400_000
        ),
        name="attend",
    )(queries, keys, values, mask_t)


def local(queries, keys, values, block_mask):
    mask_t = jnp.pad(block_mask.T, ((0, 0), (0, 112)))
    return attend(queries, keys, values, mask_t)


def solution(mesh):
    return jax.shard_map(
        local,
        mesh=mesh,
        in_specs=(P("pb", None), P(("ka", "pb"), None), P(("ka", "pb"), None), P("pb", "ka")),
        out_specs=P("pb", None),
        check_vma=False,
    )
```

```python
import jax
import jax.numpy as jnp
from jax import lax
from jax.experimental import pallas as pl
from jax.experimental.pallas import tpu as pltpu
from jax.sharding import PartitionSpec as P

HEADS = 16
HEAD_DIM = 128
BLOCK = 128
NB = 128
NPB = 8
NKA = 16
ROWS = 2048
QBLOCKS = ROWS // BLOCK
SLOTS = 8
WAVE = HEAD_DIM // 2
PACKED = ROWS // 2
HALF = PACKED // 2
PIECE = PACKED // 4
DENSE = 2 * BLOCK
MESH = pl.DeviceIdType.MESH
BF16 = jnp.bfloat16
F32 = jnp.float32
SCALE = HEAD_DIM ** (-0.5) * 1.4426950408889634
NEG = -1e30


def remote(src, dst, send, recv, pb, ka):
    return pltpu.make_async_remote_copy(
        src_ref=src,
        dst_ref=dst,
        send_sem=send,
        recv_sem=recv,
        device_id={"pb": pb, "ka": ka},
        device_id_type=MESH,
    )


def greet(peers):
    barrier = pltpu.get_barrier_semaphore()
    for pb, ka in peers:
        pl.semaphore_signal(
            barrier, inc=1, device_id={"pb": pb, "ka": ka}, device_id_type=MESH
        )
    pl.semaphore_wait(barrier, len(peers))


def xor2(a, b):
    if b == 0:
        return a
    if b == 1:
        return a + 1 - 2 * (a % 2)
    if b == 2:
        return (a + 2) % 4
    return 3 - a


def nt(a, b):
    return lax.dot_general(a, b, (((1,), (1,)), ((), ())), preferred_element_type=F32)


def attend_kernel(
    q_hbm, k_hbm, v_hbm, m_hbm, out_ref,
    got, q_ref, v_own, vt_own, kb, vb0, vb1, mb, tab_v, tab_s, p_ref, tot_ref,
    sg, pg, mg, gtot, gacc,
    sem, a_recv, z_send, z_recv, s_send, s_recv,
):
    pb = lax.axis_index("pb")
    ka = lax.axis_index("ka")
    other = pb + 1 - 2 * (pb % 2)
    up, down, far = (pb + 2) % NPB, (pb + 6) % NPB, (pb + 4) % NPB
    x, y = ka // 4, ka % 4
    vbs = (vb0, vb1)

    def cols(i):
        return pl.ds(pl.multiple_of(i * HEAD_DIM, HEAD_DIM), HEAD_DIM)

    vc = pltpu.make_async_copy(v_hbm, v_own, sem.at[0])
    vc.start()
    qc = pltpu.make_async_copy(q_hbm.at[:, cols(ka)], q_ref, sem.at[1])
    pltpu.make_async_copy(k_hbm.at[:, cols(ka)], kb.at[pb * NKA + ka], a_recv.at[0]).start()
    pltpu.make_async_copy(m_hbm, mb.at[ka], sem.at[3]).start()

    peers = [xor2(x, d // 4) * 4 + xor2(y, d % 4) for d in range(NKA)]
    greet(
        [(pb, peers[d]) for d in range(1, NKA)] + [(other, ka), (up, ka), (down, ka)]
    )

    def take(s, ref):
        remote(ref, ref, s, s, pb, ka).wait_recv()

    def half(p, w):
        return pl.ds(pl.multiple_of(p * HEAD_DIM + w * WAVE, WAVE), WAVE)

    def exchange(n, g):
        for d in range(4 * g, 4 * g + 4):
            if d:
                src = vt_own.at[half(peers[d], n - 1)] if n else k_hbm.at[:, cols(peers[d])]
                dst = (kb, vb0, vb1)[n].at[pb * NKA + ka]
                remote(src, dst, sem.at[5 + n], a_recv.at[n * 4 + g], pb, peers[d]).start()

    def turn_values():
        vc.wait()
        for h in range(HEADS):
            tile = v_own[:, h * HEAD_DIM : (h + 1) * HEAD_DIM]
            vt_own[h * HEAD_DIM : (h + 1) * HEAD_DIM, :] = tile.T
        for w in range(2):
            pltpu.make_async_copy(
                vt_own.at[half(ka, w)], vbs[w].at[pb * NKA + ka], a_recv.at[4 + 4 * w]
            ).start()

    exchange(0, 0)
    exchange(0, 1)
    for d in range(1, NKA):
        remote(m_hbm, mb.at[ka], sem.at[4], sem.at[3], pb, peers[d]).start()
    qc.start()

    bufs = (kb, vb0, vb1)

    def group(buf, who, g, first=0, count=4):
        return buf.at[pl.ds(who * NKA + xor2(x, g) * 4 + first, count)]

    NEAR, DISTANT, RELAYED = 0, 12, 24

    def send(t, kind, ref, to):
        remote(ref, ref, z_send.at[t // 4], z_recv.at[kind + t], to, ka).start()

    def own(t):
        n, g = divmod(t, 4)
        mine = group(bufs[n], pb, g)
        take(a_recv.at[t], mine)
        send(t, NEAR, mine, up)
        send(t, NEAR, mine, down)
        send(t, RELAYED, mine, other)

    def near(t):
        n, g = divmod(t, 4)
        take(z_recv.at[NEAR + t], bufs[n].at[pl.ds(0, 8)])
        send(t, DISTANT, group(bufs[n], down, g, 0, 2), up)
        send(t, DISTANT, group(bufs[n], up, g, 2, 2), down)
        send(t, RELAYED, group(bufs[n], down, g), other)
        send(t, RELAYED, group(bufs[n], up, g), other)

    def distant(t):
        n, g = divmod(t, 4)
        both = group(bufs[n], far, g)
        take(z_recv.at[DISTANT + t], both)
        send(t, RELAYED, both, other)

    def relayed(t):
        take(z_recv.at[RELAYED + t], bufs[t // 4].at[pl.ds(0, 16)])

    def make_table():
        take(sem.at[3], mb)
        live = (mb[...].reshape(NB, 128) > 0).astype(F32)
        row = lax.broadcasted_iota(jnp.int32, (NB, 128), 0)
        col = lax.broadcasted_iota(jnp.int32, (NB, 128), 1)
        lower = (col <= row).astype(F32).astype(BF16)
        rank = jnp.dot(lower, live.astype(BF16), preferred_element_type=F32)
        weight = live * ((row % NPB) * NKA + row // NPB).astype(F32)
        parts = [
            jnp.sum(jnp.where(rank == s + 1, weight, 0.0), axis=0, keepdims=True)
            for s in range(SLOTS)
        ]
        count = jnp.sum(live, axis=0, keepdims=True)
        table = jnp.concatenate(parts + [jnp.broadcast_to(count, (8, 128))], axis=0)
        tab_v[...] = table.astype(jnp.int32)
        tc = pltpu.make_async_copy(tab_v, tab_s, sem.at[2])
        tc.start()
        tc.wait()

    def place(s, i):
        return jnp.minimum(jnp.maximum(tab_s[s, i], 0), NB - 1)

    def weigh(i, carry):
        q = q_ref[pl.ds(pl.multiple_of(i * BLOCK, BLOCK), BLOCK), :]
        n = tab_s[SLOTS, i]
        ss = []
        for s in range(SLOTS):
            ss.append(nt(kb[place(s, i)], q) * SCALE + jnp.where(s < n, 0.0, NEG))
        m = ss[0]
        for s in range(1, SLOTS):
            m = jnp.maximum(m, ss[s])
        m = jnp.max(m, axis=0, keepdims=True)
        total = None
        for s in range(SLOTS):
            p = jnp.exp2(ss[s] - m)
            total = p if total is None else total + p
            p_ref[i, s] = p.astype(BF16)
        tot_ref[i] = jnp.broadcast_to(jnp.sum(total, axis=0, keepdims=True), (8, 128))
        return carry

    def gathered(w, i):
        v = jnp.concatenate([vbs[w][place(s, i)] for s in range(SLOTS)], axis=1)
        p = p_ref[i].reshape(SLOTS * BLOCK, BLOCK)
        return jnp.dot(v, p, preferred_element_type=F32) / tot_ref[i, 0:1, :]

    def value(w):
        def pair(i, carry):
            o = jnp.concatenate([gathered(w, i), gathered(w, i + 8)], axis=0)
            got[w, ka, pl.ds(pl.multiple_of(i * BLOCK, BLOCK), BLOCK), :] = o.T.astype(BF16)
            return carry

        lax.fori_loop(0, QBLOCKS // 2, pair, 0)

        @pl.when(pb == 0)
        def _():
            dense = gacc[w] / gtot[0:1, :]
            for i in range(2):
                o = dense[:, i * BLOCK : (i + 1) * BLOCK]
                o = jnp.concatenate([o, o], axis=0).T.astype(BF16)
                right = got[w, ka, i * BLOCK : (i + 1) * BLOCK, WAVE:]
                got[w, ka, i * BLOCK : (i + 1) * BLOCK, :] = jnp.concatenate(
                    [o[:, :WAVE], right], axis=1
                )

    def dense_weigh(g):
        @pl.when(pb == 0)
        def _():
            q = q_ref[0:DENSE, :]
            base = xor2(x, g) * 4

            def score(b, m):
                k = kb[pl.ds(b * NKA + base, 4)].reshape(4 * BLOCK, HEAD_DIM)
                s = nt(k, q) * SCALE
                sg[b] = s
                return jnp.maximum(m, jnp.max(s, axis=0, keepdims=True))

            old = mg[g - 1, 0:1, :] if g else jnp.full((1, DENSE), NEG, F32)
            m = lax.fori_loop(0, NPB, score, old)
            mg[g] = jnp.broadcast_to(m, (8, DENSE))

            def expo(b, total):
                p = jnp.exp2(sg[b] - m)
                pg[g, b] = p.astype(BF16)
                return total + jnp.sum(p, axis=0, keepdims=True)

            total = lax.fori_loop(0, NPB, expo, jnp.zeros((1, DENSE), F32))
            if g:
                total = total + gtot[0:1, :] * jnp.exp2(old - m)
            gtot[...] = jnp.broadcast_to(total, (8, DENSE))

    def dense_value(w, g):
        @pl.when(pb == 0)
        def _():
            base = xor2(x, g) * 4

            def part(b, acc):
                v = vbs[w][pl.ds(b * NKA + base, 4)]
                v = jnp.concatenate([v[j] for j in range(4)], axis=1)
                return acc + jnp.dot(v, pg[g, b], preferred_element_type=F32)

            acc = lax.fori_loop(0, NPB, part, jnp.zeros((WAVE, DENSE), F32))
            acc = acc * jnp.exp2(mg[g, 0:1, :] - mg[3, 0:1, :])
            gacc[w] = gacc[w] + acc if g else acc

    def at(dx, dy):
        return ((x + dx + 4) % 4) * 4 + (y + dy + 4) % 4

    class Spread:
        def __init__(self, wave):
            self.wave = wave

        def place(self, a, u, w):
            return at(u, w) if a == 0 else at(w, u)

        def ref(self, a, u, w, piece):
            lo, n = (0, 2) if piece is None else (piece, 1)
            return got.at[
                self.wave, self.place(a, u, w), pl.ds(a * HALF + lo * PIECE, n * PIECE)
            ]

        def place_id(self, u, w):
            u, w = u % 4, w % 4
            if w == 2:
                return 6 + u
            if w == 0:
                return 2 if u == 2 else 0
            return {0: 1, 3: 3, 1: 4, 2: 5}[u]

        def send(self, a, u, w, piece, du, dw):
            r = self.ref(a, u, w, piece)
            i = self.place_id(u - du, w - dw)
            remote(
                r, r, s_send.at[self.wave], s_recv.at[self.wave, i],
                pb, self.place(a, du, dw),
            ).start()

        def arrived(self, u, w):
            i = self.place_id(u, w)
            heads = {0: 2, 1: 2, 2: 1, 3: 2, 4: 2, 5: 2}.get(i, 1)
            take(s_recv.at[self.wave, i], got.at[self.wave, pl.ds(0, heads)])

        def stage(self, n):
            send, arrived = self.send, self.arrived
            both = (0, 1)
            if n == 0:
                for a in both:
                    send(a, 0, 0, None, 1, 0)
                    send(a, 0, 0, None, -1, 0)
                for a in both:
                    send(a, 0, 0, None, 0, 1)
                    send(a, 0, 0, None, 0, -1)
            elif n == 1:
                arrived(1, 0)
                for a in both:
                    send(a, -1, 0, 0, 1, 0)
                    send(a, 1, 0, 1, -1, 0)
                for a in both:
                    for u in (-1, 1):
                        send(a, u, 0, None, 0, 1)
                        send(a, u, 0, None, 0, -1)
            elif n == 2:
                arrived(0, 1)
                for a in both:
                    send(a, 0, -1, 0, 0, 1)
                    send(a, 0, 1, 1, 0, -1)
            elif n == 3:
                arrived(2, 0)
                for a in both:
                    for piece in (0, 1):
                        send(a, 2, 0, piece, 0, 1)
                        send(a, 2, 0, piece, 0, -1)
            elif n == 4:
                for u in (-1, 1):
                    arrived(u, 1)
                    for a in both:
                        send(a, u, -1, 0, 0, 1)
                        send(a, u, 1, 1, 0, -1)
            elif n == 5:
                arrived(2, 1)
                for a in both:
                    send(a, 2, -1, 0, 0, 1)
                    send(a, 2, 1, 1, 0, -1)
            else:
                for u in (0, -1, 1, 2):
                    arrived(u, 2)

    def unpack(a, u, w, piece):
        h = first.place(a, u, w)
        lo, n = (0, 2) if piece is None else (piece, 1)
        lanes = pl.ds(pl.multiple_of(h * HEAD_DIM, HEAD_DIM), HEAD_DIM)

        def rows(r, carry):
            at_row = a * HALF + lo * PIECE + r * BLOCK
            src = pl.ds(pl.multiple_of(at_row, BLOCK), BLOCK)
            low, high = got[0, h, src, :], got[1, h, src, :]
            out_ref[src, lanes] = jnp.concatenate([low[:, :WAVE], high[:, :WAVE]], axis=1)
            dst = pl.ds(pl.multiple_of(PACKED + at_row, BLOCK), BLOCK)
            out_ref[dst, lanes] = jnp.concatenate([low[:, WAVE:], high[:, WAVE:]], axis=1)
            return carry

        lax.fori_loop(0, n * PIECE // BLOCK, rows, 0)

    both = (0, 1)
    first, second = Spread(0), Spread(1)
    own(0)
    exchange(0, 2)
    own(1)
    exchange(0, 3)
    turn_values()
    near(0)
    own(2)
    exchange(1, 0)
    exchange(1, 1)
    near(1)
    own(3)
    exchange(1, 2)
    exchange(1, 3)
    distant(0)
    relayed(0)
    qc.wait()
    dense_weigh(0)
    near(2)
    distant(1)
    for g in range(4):
        exchange(2, g)
    own(4)
    make_table()
    relayed(1)
    near(3)
    own(5)
    dense_weigh(1)
    distant(2)
    relayed(2)
    near(4)
    own(6)
    dense_weigh(2)
    distant(3)
    relayed(3)
    dense_weigh(3)
    lax.fori_loop(0, 3, weigh, 0)
    own(7)
    near(5)
    distant(4)
    relayed(4)
    dense_value(0, 0)
    lax.fori_loop(3, 6, weigh, 0)
    near(6)
    distant(5)
    relayed(5)
    dense_value(0, 1)
    lax.fori_loop(6, 9, weigh, 0)
    near(7)
    own(8)
    distant(6)
    relayed(6)
    dense_value(0, 2)
    lax.fori_loop(9, 12, weigh, 0)
    distant(7)
    own(9)
    lax.fori_loop(12, 16, weigh, 0)
    relayed(7)
    dense_value(0, 3)
    value(0)
    first.stage(0)
    near(8)
    own(10)
    near(9)
    distant(8)
    relayed(8)
    dense_value(1, 0)
    own(11)
    first.stage(1)
    near(10)
    distant(9)
    relayed(9)
    dense_value(1, 1)
    near(11)
    distant(10)
    relayed(10)
    dense_value(1, 2)
    first.stage(2)
    distant(11)
    relayed(11)
    dense_value(1, 3)
    value(1)
    second.stage(0)
    for a in both:
        unpack(a, 0, 0, None)
    first.stage(3)
    first.stage(4)
    second.stage(1)
    for a in both:
        unpack(a, -1, 0, None)
        unpack(a, 1, 0, None)
    first.stage(5)
    second.stage(2)
    for a in both:
        unpack(a, 0, -1, None)
        unpack(a, 0, 1, None)
    first.stage(6)
    second.stage(3)
    for a in both:
        unpack(a, 2, 0, None)
    second.stage(4)
    for a in both:
        for u in (-1, 1):
            unpack(a, u, -1, None)
            unpack(a, u, 1, None)
    second.stage(5)
    for a in both:
        unpack(a, 2, -1, None)
        unpack(a, 2, 1, None)
    for u in (0, -1, 1, 2):
        second.arrived(u, 2)
        for a in both:
            unpack(a, u, 2, None)
    for s, ref in (
        (sem.at[4], mb.at[pl.ds(0, NKA - 1)]),
        (sem.at[5], kb.at[pl.ds(0, NKA - 1)]),
        (sem.at[6], vb0.at[pl.ds(0, NKA - 1)]),
        (sem.at[7], vb1.at[pl.ds(0, NKA - 1)]),
        (z_send.at[0], kb.at[pl.ds(0, 112)]),
        (z_send.at[1], vb0.at[pl.ds(0, 112)]),
        (z_send.at[2], vb1.at[pl.ds(0, 112)]),
        (s_send.at[0], got.at[0, pl.ds(0, NKA - 1)]),
        (s_send.at[1], got.at[1, pl.ds(0, NKA - 1)]),
    ):
        remote(ref, ref, s, s, pb, ka).wait_send()


def attend(queries, keys, values, mask_t):
    any_spec = pl.BlockSpec(memory_space=pltpu.HBM)
    dma = pltpu.SemaphoreType.DMA
    vmem = pltpu.VMEM
    return pl.pallas_call(
        attend_kernel,
        out_shape=pltpu.VMEM((ROWS, HEADS * HEAD_DIM), BF16),
        in_specs=[any_spec] * 4,
        out_specs=pl.BlockSpec(memory_space=pltpu.VMEM),
        scratch_shapes=[
            vmem((2, NKA, PACKED, 128), BF16),
            vmem((ROWS, HEAD_DIM), BF16),
            vmem((BLOCK, HEADS * HEAD_DIM), BF16),
            vmem((HEADS * HEAD_DIM, BLOCK), BF16),
            vmem((NB, BLOCK, HEAD_DIM), BF16),
            vmem((NB, WAVE, BLOCK), BF16),
            vmem((NB, WAVE, BLOCK), BF16),
            vmem((NKA, 8, 128), jnp.int32),
            vmem((16, 128), jnp.int32),
            pltpu.SMEM((16, 128), jnp.int32),
            vmem((QBLOCKS, SLOTS, BLOCK, BLOCK), BF16),
            vmem((QBLOCKS, 8, 128), F32),
            vmem((NPB, 4 * BLOCK, DENSE), F32),
            vmem((4, NPB, 4 * BLOCK, DENSE), BF16),
            vmem((4, 8, DENSE), F32),
            vmem((8, DENSE), F32),
            vmem((2, WAVE, DENSE), F32),
            dma((8,)), dma((12,)), dma((3,)), dma((36,)), dma((2,)), dma((2, 10)),
        ],
        compiler_params=pltpu.CompilerParams(
            collective_id=0, has_side_effects=True, vmem_limit_bytes=58_400_000
        ),
        name="attend",
    )(queries, keys, values, mask_t)


def local(queries, keys, values, block_mask):
    mask_t = jnp.pad(block_mask.T, ((0, 0), (0, 112)))
    return attend(queries, keys, values, mask_t)


def solution(mesh):
    return jax.shard_map(
        local,
        mesh=mesh,
        in_specs=(P("pb", None), P(("ka", "pb"), None), P(("ka", "pb"), None), P("pb", "ka")),
        out_specs=P("pb", None),
        check_vma=False,
    )
```

```python
import jax
import jax.numpy as jnp
from jax import lax
from jax.experimental import pallas as pl
from jax.experimental.pallas import tpu as pltpu
from jax.sharding import PartitionSpec as P

HEADS = 16
HEAD_DIM = 128
BLOCK = 128
NB = 128
NPB = 8
NKA = 16
ROWS = 2048
QBLOCKS = ROWS // BLOCK
SLOTS = 8
WAVE = HEAD_DIM // 2
PACKED = ROWS // 2
HALF = PACKED // 2
PIECE = PACKED // 4
DENSE = 2 * BLOCK
MESH = pl.DeviceIdType.MESH
BF16 = jnp.bfloat16
F32 = jnp.float32
SCALE = HEAD_DIM ** (-0.5) * 1.4426950408889634
NEG = -1e30


def remote(src, dst, send, recv, pb, ka):
    return pltpu.make_async_remote_copy(
        src_ref=src,
        dst_ref=dst,
        send_sem=send,
        recv_sem=recv,
        device_id={"pb": pb, "ka": ka},
        device_id_type=MESH,
    )


def greet(peers):
    barrier = pltpu.get_barrier_semaphore()
    for pb, ka in peers:
        pl.semaphore_signal(
            barrier, inc=1, device_id={"pb": pb, "ka": ka}, device_id_type=MESH
        )
    pl.semaphore_wait(barrier, len(peers))


def xor2(a, b):
    if b == 0:
        return a
    if b == 1:
        return a + 1 - 2 * (a % 2)
    if b == 2:
        return (a + 2) % 4
    return 3 - a


def nt(a, b):
    return lax.dot_general(a, b, (((1,), (1,)), ((), ())), preferred_element_type=F32)


def attend_kernel(
    q_hbm, k_hbm, v_hbm, m_hbm, out_ref,
    got, q_ref, v_own, vt_own, kb, vb0, vb1, mb, tab_v, tab_s, p_ref, tot_ref,
    sg, pg, mg, gtot, gacc,
    sem, a_recv, z_send, z_recv, s_send, s_recv,
):
    pb = lax.axis_index("pb")
    ka = lax.axis_index("ka")
    other = pb + 1 - 2 * (pb % 2)
    up, down, far = (pb + 2) % NPB, (pb + 6) % NPB, (pb + 4) % NPB
    x, y = ka // 4, ka % 4
    vbs = (vb0, vb1)

    def cols(i):
        return pl.ds(pl.multiple_of(i * HEAD_DIM, HEAD_DIM), HEAD_DIM)

    vc = pltpu.make_async_copy(v_hbm, v_own, sem.at[0])
    vc.start()
    qc = pltpu.make_async_copy(q_hbm.at[:, cols(ka)], q_ref, sem.at[1])
    pltpu.make_async_copy(k_hbm.at[:, cols(ka)], kb.at[pb * NKA + ka], a_recv.at[0]).start()
    pltpu.make_async_copy(m_hbm, mb.at[ka], sem.at[3]).start()

    peers = [xor2(x, d // 4) * 4 + xor2(y, d % 4) for d in range(NKA)]
    greet(
        [(pb, peers[d]) for d in range(1, NKA)] + [(other, ka), (up, ka), (down, ka)]
    )

    def take(s, ref):
        remote(ref, ref, s, s, pb, ka).wait_recv()

    def half(p, w):
        return pl.ds(pl.multiple_of(p * HEAD_DIM + w * WAVE, WAVE), WAVE)

    def exchange(n, g):
        for d in range(4 * g, 4 * g + 4):
            if d:
                src = vt_own.at[half(peers[d], n - 1)] if n else k_hbm.at[:, cols(peers[d])]
                dst = (kb, vb0, vb1)[n].at[pb * NKA + ka]
                remote(src, dst, sem.at[5 + n], a_recv.at[n * 4 + g], pb, peers[d]).start()

    def turn_values():
        vc.wait()
        for h in range(HEADS):
            tile = v_own[:, h * HEAD_DIM : (h + 1) * HEAD_DIM]
            vt_own[h * HEAD_DIM : (h + 1) * HEAD_DIM, :] = tile.T
        for w in range(2):
            pltpu.make_async_copy(
                vt_own.at[half(ka, w)], vbs[w].at[pb * NKA + ka], a_recv.at[4 + 4 * w]
            ).start()

    exchange(0, 0)
    exchange(0, 1)
    for d in range(1, NKA):
        remote(m_hbm, mb.at[ka], sem.at[4], sem.at[3], pb, peers[d]).start()
    qc.start()

    bufs = (kb, vb0, vb1)

    def group(buf, who, g, first=0, count=4):
        return buf.at[pl.ds(who * NKA + xor2(x, g) * 4 + first, count)]

    NEAR, DISTANT, RELAYED = 0, 12, 24

    def send(t, kind, ref, to):
        remote(ref, ref, z_send.at[t // 4], z_recv.at[kind + t], to, ka).start()

    def own(t):
        n, g = divmod(t, 4)
        mine = group(bufs[n], pb, g)
        take(a_recv.at[t], mine)
        send(t, NEAR, mine, up)
        send(t, NEAR, mine, down)
        send(t, RELAYED, mine, other)

    def near(t):
        n, g = divmod(t, 4)
        take(z_recv.at[NEAR + t], bufs[n].at[pl.ds(0, 8)])
        send(t, DISTANT, group(bufs[n], down, g, 0, 2), up)
        send(t, DISTANT, group(bufs[n], up, g, 2, 2), down)
        send(t, RELAYED, group(bufs[n], down, g), other)
        send(t, RELAYED, group(bufs[n], up, g), other)

    def distant(t):
        n, g = divmod(t, 4)
        both = group(bufs[n], far, g)
        take(z_recv.at[DISTANT + t], both)
        send(t, RELAYED, both, other)

    def relayed(t):
        take(z_recv.at[RELAYED + t], bufs[t // 4].at[pl.ds(0, 16)])

    def make_table():
        take(sem.at[3], mb)
        live = (mb[...].reshape(NB, 128) > 0).astype(F32)
        row = lax.broadcasted_iota(jnp.int32, (NB, 128), 0)
        col = lax.broadcasted_iota(jnp.int32, (NB, 128), 1)
        lower = (col <= row).astype(F32).astype(BF16)
        rank = jnp.dot(lower, live.astype(BF16), preferred_element_type=F32)
        weight = live * ((row % NPB) * NKA + row // NPB).astype(F32)
        parts = [
            jnp.sum(jnp.where(rank == s + 1, weight, 0.0), axis=0, keepdims=True)
            for s in range(SLOTS)
        ]
        count = jnp.sum(live, axis=0, keepdims=True)
        table = jnp.concatenate(parts + [jnp.broadcast_to(count, (8, 128))], axis=0)
        tab_v[...] = table.astype(jnp.int32)
        tc = pltpu.make_async_copy(tab_v, tab_s, sem.at[2])
        tc.start()
        tc.wait()

    def place(s, i):
        return jnp.minimum(jnp.maximum(tab_s[s, i], 0), NB - 1)

    def weigh(i, carry):
        q = q_ref[pl.ds(pl.multiple_of(i * BLOCK, BLOCK), BLOCK), :]
        n = tab_s[SLOTS, i]
        ss = []
        for s in range(SLOTS):
            ss.append(nt(kb[place(s, i)], q) * SCALE + jnp.where(s < n, 0.0, NEG))
        m = ss[0]
        for s in range(1, SLOTS):
            m = jnp.maximum(m, ss[s])
        m = jnp.max(m, axis=0, keepdims=True)
        total = None
        for s in range(SLOTS):
            p = jnp.exp2(ss[s] - m)
            total = p if total is None else total + p
            p_ref[i, s] = p.astype(BF16)
        tot_ref[i] = jnp.broadcast_to(jnp.sum(total, axis=0, keepdims=True), (8, 128))
        return carry

    def gathered(w, i):
        v = jnp.concatenate([vbs[w][place(s, i)] for s in range(SLOTS)], axis=1)
        p = p_ref[i].reshape(SLOTS * BLOCK, BLOCK)
        return jnp.dot(v, p, preferred_element_type=F32) / tot_ref[i, 0:1, :]

    def value(w):
        def pair(i, carry):
            o = jnp.concatenate([gathered(w, i), gathered(w, i + 8)], axis=0)
            got[w, ka, pl.ds(pl.multiple_of(i * BLOCK, BLOCK), BLOCK), :] = o.T.astype(BF16)
            return carry

        lax.fori_loop(0, QBLOCKS // 2, pair, 0)

        @pl.when(pb == 0)
        def _():
            dense = gacc[w] / gtot[0:1, :]
            for i in range(2):
                o = dense[:, i * BLOCK : (i + 1) * BLOCK]
                o = jnp.concatenate([o, o], axis=0).T.astype(BF16)
                right = got[w, ka, i * BLOCK : (i + 1) * BLOCK, WAVE:]
                got[w, ka, i * BLOCK : (i + 1) * BLOCK, :] = jnp.concatenate(
                    [o[:, :WAVE], right], axis=1
                )

    def dense_weigh(g):
        @pl.when(pb == 0)
        def _():
            q = q_ref[0:DENSE, :]
            base = xor2(x, g) * 4

            def score(b, m):
                k = kb[pl.ds(b * NKA + base, 4)].reshape(4 * BLOCK, HEAD_DIM)
                s = nt(k, q) * SCALE
                sg[b] = s
                return jnp.maximum(m, jnp.max(s, axis=0, keepdims=True))

            old = mg[g - 1, 0:1, :] if g else jnp.full((1, DENSE), NEG, F32)
            m = lax.fori_loop(0, NPB, score, old)
            mg[g] = jnp.broadcast_to(m, (8, DENSE))

            def expo(b, total):
                p = jnp.exp2(sg[b] - m)
                pg[g, b] = p.astype(BF16)
                return total + jnp.sum(p, axis=0, keepdims=True)

            total = lax.fori_loop(0, NPB, expo, jnp.zeros((1, DENSE), F32))
            if g:
                total = total + gtot[0:1, :] * jnp.exp2(old - m)
            gtot[...] = jnp.broadcast_to(total, (8, DENSE))

    def dense_value(w, g):
        @pl.when(pb == 0)
        def _():
            base = xor2(x, g) * 4

            def part(b, acc):
                v = vbs[w][pl.ds(b * NKA + base, 4)]
                v = jnp.concatenate([v[j] for j in range(4)], axis=1)
                return acc + jnp.dot(v, pg[g, b], preferred_element_type=F32)

            acc = lax.fori_loop(0, NPB, part, jnp.zeros((WAVE, DENSE), F32))
            acc = acc * jnp.exp2(mg[g, 0:1, :] - mg[3, 0:1, :])
            gacc[w] = gacc[w] + acc if g else acc

    def at(dx, dy):
        return ((x + dx + 4) % 4) * 4 + (y + dy + 4) % 4

    class Spread:
        def __init__(self, wave):
            self.wave = wave

        def place(self, a, u, w):
            return at(u, w) if a == 0 else at(w, u)

        def ref(self, a, u, w, piece):
            lo, n = (0, 2) if piece is None else (piece, 1)
            return got.at[
                self.wave, self.place(a, u, w), pl.ds(a * HALF + lo * PIECE, n * PIECE)
            ]

        def place_id(self, u, w):
            u, w = u % 4, w % 4
            if w == 2:
                return 6 + u
            if w == 0:
                return 2 if u == 2 else 0
            return {0: 1, 3: 3, 1: 4, 2: 5}[u]

        def send(self, a, u, w, piece, du, dw):
            r = self.ref(a, u, w, piece)
            i = self.place_id(u - du, w - dw)
            remote(
                r, r, s_send.at[self.wave], s_recv.at[self.wave, i],
                pb, self.place(a, du, dw),
            ).start()

        def arrived(self, u, w):
            i = self.place_id(u, w)
            heads = {0: 2, 1: 2, 2: 1, 3: 2, 4: 2, 5: 2}.get(i, 1)
            take(s_recv.at[self.wave, i], got.at[self.wave, pl.ds(0, heads)])

        def stage(self, n):
            send, arrived = self.send, self.arrived
            both = (0, 1)
            if n == 0:
                for a in both:
                    send(a, 0, 0, None, 1, 0)
                    send(a, 0, 0, None, -1, 0)
                for a in both:
                    send(a, 0, 0, None, 0, 1)
                    send(a, 0, 0, None, 0, -1)
            elif n == 1:
                arrived(1, 0)
                for a in both:
                    send(a, -1, 0, 0, 1, 0)
                    send(a, 1, 0, 1, -1, 0)
                for a in both:
                    for u in (-1, 1):
                        send(a, u, 0, None, 0, 1)
                        send(a, u, 0, None, 0, -1)
            elif n == 2:
                arrived(0, 1)
                for a in both:
                    send(a, 0, -1, 0, 0, 1)
                    send(a, 0, 1, 1, 0, -1)
            elif n == 3:
                arrived(2, 0)
                for a in both:
                    for piece in (0, 1):
                        send(a, 2, 0, piece, 0, 1)
                        send(a, 2, 0, piece, 0, -1)
            elif n == 4:
                for u in (-1, 1):
                    arrived(u, 1)
                    for a in both:
                        send(a, u, -1, 0, 0, 1)
                        send(a, u, 1, 1, 0, -1)
            elif n == 5:
                arrived(2, 1)
                for a in both:
                    send(a, 2, -1, 0, 0, 1)
                    send(a, 2, 1, 1, 0, -1)
            else:
                for u in (0, -1, 1, 2):
                    arrived(u, 2)

    def unpack(a, u, w, piece):
        h = first.place(a, u, w)
        lo, n = (0, 2) if piece is None else (piece, 1)
        lanes = pl.ds(pl.multiple_of(h * HEAD_DIM, HEAD_DIM), HEAD_DIM)

        def rows(r, carry):
            at_row = a * HALF + lo * PIECE + r * BLOCK
            src = pl.ds(pl.multiple_of(at_row, BLOCK), BLOCK)
            low, high = got[0, h, src, :], got[1, h, src, :]
            out_ref[src, lanes] = jnp.concatenate([low[:, :WAVE], high[:, :WAVE]], axis=1)
            dst = pl.ds(pl.multiple_of(PACKED + at_row, BLOCK), BLOCK)
            out_ref[dst, lanes] = jnp.concatenate([low[:, WAVE:], high[:, WAVE:]], axis=1)
            return carry

        lax.fori_loop(0, n * PIECE // BLOCK, rows, 0)

    both = (0, 1)
    first, second = Spread(0), Spread(1)
    own(0)
    exchange(0, 2)
    own(1)
    exchange(0, 3)
    turn_values()
    near(0)
    own(2)
    exchange(1, 0)
    exchange(1, 1)
    near(1)
    own(3)
    exchange(1, 2)
    exchange(1, 3)
    distant(0)
    relayed(0)
    qc.wait()
    dense_weigh(0)
    near(2)
    distant(1)
    for g in range(4):
        exchange(2, g)
    own(4)
    make_table()
    relayed(1)
    near(3)
    own(5)
    dense_weigh(1)
    distant(2)
    relayed(2)
    near(4)
    own(6)
    dense_weigh(2)
    distant(3)
    relayed(3)
    dense_weigh(3)
    lax.fori_loop(0, 3, weigh, 0)
    own(7)
    near(5)
    distant(4)
    relayed(4)
    dense_value(0, 0)
    lax.fori_loop(3, 6, weigh, 0)
    near(6)
    distant(5)
    relayed(5)
    dense_value(0, 1)
    lax.fori_loop(6, 9, weigh, 0)
    near(7)
    own(8)
    distant(6)
    relayed(6)
    dense_value(0, 2)
    lax.fori_loop(9, 12, weigh, 0)
    distant(7)
    own(9)
    lax.fori_loop(12, 16, weigh, 0)
    relayed(7)
    dense_value(0, 3)
    value(0)
    first.stage(0)
    near(8)
    own(10)
    near(9)
    distant(8)
    own(11)
    near(10)
    distant(9)
    first.stage(1)
    near(11)
    distant(10)
    first.stage(2)
    distant(11)
    first.stage(3)
    for g in range(4):
        relayed(8 + g)
        dense_value(1, g)
    first.stage(4)
    value(1)
    second.stage(0)
    for a in both:
        unpack(a, 0, 0, None)
    second.stage(1)
    for a in both:
        unpack(a, -1, 0, None)
        unpack(a, 1, 0, None)
    first.stage(5)
    second.stage(2)
    for a in both:
        unpack(a, 0, -1, None)
        unpack(a, 0, 1, None)
    first.stage(6)
    second.stage(3)
    for a in both:
        unpack(a, 2, 0, None)
    second.stage(4)
    for a in both:
        for u in (-1, 1):
            unpack(a, u, -1, None)
            unpack(a, u, 1, None)
    second.stage(5)
    for a in both:
        unpack(a, 2, -1, None)
        unpack(a, 2, 1, None)
    for u in (0, -1, 1, 2):
        second.arrived(u, 2)
        for a in both:
            unpack(a, u, 2, None)
    for s, ref in (
        (sem.at[4], mb.at[pl.ds(0, NKA - 1)]),
        (sem.at[5], kb.at[pl.ds(0, NKA - 1)]),
        (sem.at[6], vb0.at[pl.ds(0, NKA - 1)]),
        (sem.at[7], vb1.at[pl.ds(0, NKA - 1)]),
        (z_send.at[0], kb.at[pl.ds(0, 112)]),
        (z_send.at[1], vb0.at[pl.ds(0, 112)]),
        (z_send.at[2], vb1.at[pl.ds(0, 112)]),
        (s_send.at[0], got.at[0, pl.ds(0, NKA - 1)]),
        (s_send.at[1], got.at[1, pl.ds(0, NKA - 1)]),
    ):
        remote(ref, ref, s, s, pb, ka).wait_send()


def attend(queries, keys, values, mask_t):
    any_spec = pl.BlockSpec(memory_space=pltpu.HBM)
    dma = pltpu.SemaphoreType.DMA
    vmem = pltpu.VMEM
    return pl.pallas_call(
        attend_kernel,
        out_shape=pltpu.VMEM((ROWS, HEADS * HEAD_DIM), BF16),
        in_specs=[any_spec] * 4,
        out_specs=pl.BlockSpec(memory_space=pltpu.VMEM),
        scratch_shapes=[
            vmem((2, NKA, PACKED, 128), BF16),
            vmem((ROWS, HEAD_DIM), BF16),
            vmem((BLOCK, HEADS * HEAD_DIM), BF16),
            vmem((HEADS * HEAD_DIM, BLOCK), BF16),
            vmem((NB, BLOCK, HEAD_DIM), BF16),
            vmem((NB, WAVE, BLOCK), BF16),
            vmem((NB, WAVE, BLOCK), BF16),
            vmem((NKA, 8, 128), jnp.int32),
            vmem((16, 128), jnp.int32),
            pltpu.SMEM((16, 128), jnp.int32),
            vmem((QBLOCKS, SLOTS, BLOCK, BLOCK), BF16),
            vmem((QBLOCKS, 8, 128), F32),
            vmem((NPB, 4 * BLOCK, DENSE), F32),
            vmem((4, NPB, 4 * BLOCK, DENSE), BF16),
            vmem((4, 8, DENSE), F32),
            vmem((8, DENSE), F32),
            vmem((2, WAVE, DENSE), F32),
            dma((8,)), dma((12,)), dma((3,)), dma((36,)), dma((2,)), dma((2, 10)),
        ],
        compiler_params=pltpu.CompilerParams(
            collective_id=0, has_side_effects=True, vmem_limit_bytes=58_400_000
        ),
        name="attend",
    )(queries, keys, values, mask_t)


def local(queries, keys, values, block_mask):
    mask_t = jnp.pad(block_mask.T, ((0, 0), (0, 112)))
    return attend(queries, keys, values, mask_t)


def solution(mesh):
    return jax.shard_map(
        local,
        mesh=mesh,
        in_specs=(P("pb", None), P(("ka", "pb"), None), P(("ka", "pb"), None), P("pb", "ka")),
        out_specs=P("pb", None),
        check_vma=False,
    )
```

```python
import jax
import jax.numpy as jnp
from jax import lax
from jax.experimental import pallas as pl
from jax.experimental.pallas import tpu as pltpu
from jax.sharding import PartitionSpec as P

HEADS = 16
HEAD_DIM = 128
BLOCK = 128
NB = 128
NPB = 8
NKA = 16
ROWS = 2048
QBLOCKS = ROWS // BLOCK
SLOTS = 8
WAVE = HEAD_DIM // 2
PACKED = ROWS // 2
HALF = PACKED // 2
PIECE = PACKED // 4
DENSE = 2 * BLOCK
MESH = pl.DeviceIdType.MESH
BF16 = jnp.bfloat16
F32 = jnp.float32
SCALE = HEAD_DIM ** (-0.5) * 1.4426950408889634
NEG = -1e30


def remote(src, dst, send, recv, pb, ka):
    return pltpu.make_async_remote_copy(
        src_ref=src,
        dst_ref=dst,
        send_sem=send,
        recv_sem=recv,
        device_id={"pb": pb, "ka": ka},
        device_id_type=MESH,
    )


def greet(peers):
    barrier = pltpu.get_barrier_semaphore()
    for pb, ka in peers:
        pl.semaphore_signal(
            barrier, inc=1, device_id={"pb": pb, "ka": ka}, device_id_type=MESH
        )
    pl.semaphore_wait(barrier, len(peers))


def xor2(a, b):
    if b == 0:
        return a
    if b == 1:
        return a + 1 - 2 * (a % 2)
    if b == 2:
        return (a + 2) % 4
    return 3 - a


def nt(a, b):
    return lax.dot_general(a, b, (((1,), (1,)), ((), ())), preferred_element_type=F32)


def attend_kernel(
    q_hbm, k_hbm, v_hbm, m_hbm, out_ref,
    got, q_ref, v_own, vt_own, kb, vb0, vb1, mb, tab_v, tab_s, p_ref, tot_ref,
    sg, pg, mg, gtot, gacc,
    sem, a_recv, z_send, z_recv, s_send, s_recv,
):
    pb = lax.axis_index("pb")
    ka = lax.axis_index("ka")
    other = pb + 1 - 2 * (pb % 2)
    up, down, far = (pb + 2) % NPB, (pb + 6) % NPB, (pb + 4) % NPB
    x, y = ka // 4, ka % 4
    vbs = (vb0, vb1)

    def cols(i):
        return pl.ds(pl.multiple_of(i * HEAD_DIM, HEAD_DIM), HEAD_DIM)

    vc = pltpu.make_async_copy(v_hbm, v_own, sem.at[0])
    vc.start()
    qc = pltpu.make_async_copy(q_hbm.at[:, cols(ka)], q_ref, sem.at[1])
    pltpu.make_async_copy(k_hbm.at[:, cols(ka)], kb.at[pb * NKA + ka], a_recv.at[0]).start()
    pltpu.make_async_copy(m_hbm, mb.at[ka], sem.at[3]).start()

    peers = [xor2(x, d // 4) * 4 + xor2(y, d % 4) for d in range(NKA)]
    greet(
        [(pb, peers[d]) for d in range(1, NKA)] + [(other, ka), (up, ka), (down, ka)]
    )

    def take(s, ref):
        remote(ref, ref, s, s, pb, ka).wait_recv()

    def half(p, w):
        return pl.ds(pl.multiple_of(p * HEAD_DIM + w * WAVE, WAVE), WAVE)

    def exchange(n, g):
        for d in range(4 * g, 4 * g + 4):
            if d:
                src = vt_own.at[half(peers[d], n - 1)] if n else k_hbm.at[:, cols(peers[d])]
                dst = (kb, vb0, vb1)[n].at[pb * NKA + ka]
                remote(src, dst, sem.at[5 + n], a_recv.at[n * 4 + g], pb, peers[d]).start()

    def turn_values():
        vc.wait()
        for h in range(HEADS):
            tile = v_own[:, h * HEAD_DIM : (h + 1) * HEAD_DIM]
            vt_own[h * HEAD_DIM : (h + 1) * HEAD_DIM, :] = tile.T
        for w in range(2):
            pltpu.make_async_copy(
                vt_own.at[half(ka, w)], vbs[w].at[pb * NKA + ka], a_recv.at[4 + 4 * w]
            ).start()

    exchange(0, 0)
    exchange(0, 1)
    for d in range(1, NKA):
        remote(m_hbm, mb.at[ka], sem.at[4], sem.at[3], pb, peers[d]).start()
    qc.start()

    bufs = (kb, vb0, vb1)

    def group(buf, who, g, first=0, count=4):
        return buf.at[pl.ds(who * NKA + xor2(x, g) * 4 + first, count)]

    NEAR, DISTANT, RELAYED = 0, 12, 24

    def send(t, kind, ref, to):
        remote(ref, ref, z_send.at[t // 4], z_recv.at[kind + t], to, ka).start()

    def own(t):
        n, g = divmod(t, 4)
        mine = group(bufs[n], pb, g)
        take(a_recv.at[t], mine)
        send(t, NEAR, mine, up)
        send(t, NEAR, mine, down)
        send(t, RELAYED, mine, other)

    def near(t):
        n, g = divmod(t, 4)
        take(z_recv.at[NEAR + t], bufs[n].at[pl.ds(0, 8)])
        send(t, DISTANT, group(bufs[n], down, g, 0, 2), up)
        send(t, DISTANT, group(bufs[n], up, g, 2, 2), down)
        send(t, RELAYED, group(bufs[n], down, g), other)
        send(t, RELAYED, group(bufs[n], up, g), other)

    def distant(t):
        n, g = divmod(t, 4)
        both = group(bufs[n], far, g)
        take(z_recv.at[DISTANT + t], both)
        send(t, RELAYED, both, other)

    def relayed(t):
        take(z_recv.at[RELAYED + t], bufs[t // 4].at[pl.ds(0, 16)])

    def make_table():
        take(sem.at[3], mb)
        live = (mb[...].reshape(NB, 128) > 0).astype(F32)
        row = lax.broadcasted_iota(jnp.int32, (NB, 128), 0)
        col = lax.broadcasted_iota(jnp.int32, (NB, 128), 1)
        lower = (col <= row).astype(F32).astype(BF16)
        rank = jnp.dot(lower, live.astype(BF16), preferred_element_type=F32)
        weight = live * ((row % NPB) * NKA + row // NPB).astype(F32)
        parts = [
            jnp.sum(jnp.where(rank == s + 1, weight, 0.0), axis=0, keepdims=True)
            for s in range(SLOTS)
        ]
        count = jnp.sum(live, axis=0, keepdims=True)
        table = jnp.concatenate(parts + [jnp.broadcast_to(count, (8, 128))], axis=0)
        tab_v[...] = table.astype(jnp.int32)
        tc = pltpu.make_async_copy(tab_v, tab_s, sem.at[2])
        tc.start()
        tc.wait()

    def place(s, i):
        return jnp.minimum(jnp.maximum(tab_s[s, i], 0), NB - 1)

    def weigh(i, carry):
        q = q_ref[pl.ds(pl.multiple_of(i * BLOCK, BLOCK), BLOCK), :]
        n = tab_s[SLOTS, i]
        ss = []
        for s in range(SLOTS):
            ss.append(nt(kb[place(s, i)], q) * SCALE + jnp.where(s < n, 0.0, NEG))
        m = ss[0]
        for s in range(1, SLOTS):
            m = jnp.maximum(m, ss[s])
        m = jnp.max(m, axis=0, keepdims=True)
        total = None
        for s in range(SLOTS):
            p = jnp.exp2(ss[s] - m)
            total = p if total is None else total + p
            p_ref[i, s] = p.astype(BF16)
        tot_ref[i] = jnp.broadcast_to(jnp.sum(total, axis=0, keepdims=True), (8, 128))
        return carry

    def gathered(w, i):
        v = jnp.concatenate([vbs[w][place(s, i)] for s in range(SLOTS)], axis=1)
        p = p_ref[i].reshape(SLOTS * BLOCK, BLOCK)
        return jnp.dot(v, p, preferred_element_type=F32) / tot_ref[i, 0:1, :]

    def value(w):
        def pair(i, carry):
            o = jnp.concatenate([gathered(w, i), gathered(w, i + 8)], axis=0)
            got[w, ka, pl.ds(pl.multiple_of(i * BLOCK, BLOCK), BLOCK), :] = o.T.astype(BF16)
            return carry

        lax.fori_loop(0, QBLOCKS // 2, pair, 0)

        @pl.when(pb == 0)
        def _():
            dense = gacc[w] / gtot[0:1, :]
            for i in range(2):
                o = dense[:, i * BLOCK : (i + 1) * BLOCK]
                o = jnp.concatenate([o, o], axis=0).T.astype(BF16)
                right = got[w, ka, i * BLOCK : (i + 1) * BLOCK, WAVE:]
                got[w, ka, i * BLOCK : (i + 1) * BLOCK, :] = jnp.concatenate(
                    [o[:, :WAVE], right], axis=1
                )

    def dense_weigh(g):
        @pl.when(pb == 0)
        def _():
            q = q_ref[0:DENSE, :]
            base = xor2(x, g) * 4

            def score(b, m):
                k = kb[pl.ds(b * NKA + base, 4)].reshape(4 * BLOCK, HEAD_DIM)
                s = nt(k, q) * SCALE
                sg[b] = s
                return jnp.maximum(m, jnp.max(s, axis=0, keepdims=True))

            old = mg[g - 1, 0:1, :] if g else jnp.full((1, DENSE), NEG, F32)
            m = lax.fori_loop(0, NPB, score, old)
            mg[g] = jnp.broadcast_to(m, (8, DENSE))

            def expo(b, total):
                p = jnp.exp2(sg[b] - m)
                pg[g, b] = p.astype(BF16)
                return total + jnp.sum(p, axis=0, keepdims=True)

            total = lax.fori_loop(0, NPB, expo, jnp.zeros((1, DENSE), F32))
            if g:
                total = total + gtot[0:1, :] * jnp.exp2(old - m)
            gtot[...] = jnp.broadcast_to(total, (8, DENSE))

    def dense_value(w, g):
        @pl.when(pb == 0)
        def _():
            base = xor2(x, g) * 4

            def part(b, acc):
                v = vbs[w][pl.ds(b * NKA + base, 4)]
                v = jnp.concatenate([v[j] for j in range(4)], axis=1)
                return acc + jnp.dot(v, pg[g, b], preferred_element_type=F32)

            acc = lax.fori_loop(0, NPB, part, jnp.zeros((WAVE, DENSE), F32))
            acc = acc * jnp.exp2(mg[g, 0:1, :] - mg[3, 0:1, :])
            gacc[w] = gacc[w] + acc if g else acc

    def at(dx, dy):
        return ((x + dx + 4) % 4) * 4 + (y + dy + 4) % 4

    class Spread:
        def __init__(self, wave):
            self.wave = wave

        def place(self, a, u, w):
            return at(u, w) if a == 0 else at(w, u)

        def ref(self, a, u, w, piece):
            lo, n = (0, 2) if piece is None else (piece, 1)
            return got.at[
                self.wave, self.place(a, u, w), pl.ds(a * HALF + lo * PIECE, n * PIECE)
            ]

        def place_id(self, u, w):
            u, w = u % 4, w % 4
            if w == 2:
                return 6 + u
            if w == 0:
                return 2 if u == 2 else 0
            return {0: 1, 3: 3, 1: 4, 2: 5}[u]

        def send(self, a, u, w, piece, du, dw):
            r = self.ref(a, u, w, piece)
            i = self.place_id(u - du, w - dw)
            remote(
                r, r, s_send.at[self.wave], s_recv.at[self.wave, i],
                pb, self.place(a, du, dw),
            ).start()

        def arrived(self, u, w):
            i = self.place_id(u, w)
            heads = {0: 2, 1: 2, 2: 1, 3: 2, 4: 2, 5: 2}.get(i, 1)
            take(s_recv.at[self.wave, i], got.at[self.wave, pl.ds(0, heads)])

        def stage(self, n):
            send, arrived = self.send, self.arrived
            both = (0, 1)
            if n == 0:
                for a in both:
                    send(a, 0, 0, None, 1, 0)
                    send(a, 0, 0, None, -1, 0)
                for a in both:
                    send(a, 0, 0, None, 0, 1)
                    send(a, 0, 0, None, 0, -1)
            elif n == 1:
                arrived(1, 0)
                for a in both:
                    send(a, -1, 0, 0, 1, 0)
                    send(a, 1, 0, 1, -1, 0)
                for a in both:
                    for u in (-1, 1):
                        send(a, u, 0, None, 0, 1)
                        send(a, u, 0, None, 0, -1)
            elif n == 2:
                arrived(0, 1)
                for a in both:
                    send(a, 0, -1, 0, 0, 1)
                    send(a, 0, 1, 1, 0, -1)
            elif n == 3:
                arrived(2, 0)
                for a in both:
                    for piece in (0, 1):
                        send(a, 2, 0, piece, 0, 1)
                        send(a, 2, 0, piece, 0, -1)
            elif n == 4:
                for u in (-1, 1):
                    arrived(u, 1)
                    for a in both:
                        send(a, u, -1, 0, 0, 1)
                        send(a, u, 1, 1, 0, -1)
            elif n == 5:
                arrived(2, 1)
                for a in both:
                    send(a, 2, -1, 0, 0, 1)
                    send(a, 2, 1, 1, 0, -1)
            else:
                for u in (0, -1, 1, 2):
                    arrived(u, 2)

    def unpack(a, u, w, piece):
        h = first.place(a, u, w)
        lo, n = (0, 2) if piece is None else (piece, 1)
        lanes = pl.ds(pl.multiple_of(h * HEAD_DIM, HEAD_DIM), HEAD_DIM)

        def rows(r, carry):
            at_row = a * HALF + lo * PIECE + r * BLOCK
            src = pl.ds(pl.multiple_of(at_row, BLOCK), BLOCK)
            low, high = got[0, h, src, :], got[1, h, src, :]
            out_ref[src, lanes] = jnp.concatenate([low[:, :WAVE], high[:, :WAVE]], axis=1)
            dst = pl.ds(pl.multiple_of(PACKED + at_row, BLOCK), BLOCK)
            out_ref[dst, lanes] = jnp.concatenate([low[:, WAVE:], high[:, WAVE:]], axis=1)
            return carry

        lax.fori_loop(0, n * PIECE // BLOCK, rows, 0)

    both = (0, 1)
    first, second = Spread(0), Spread(1)
    own(0)
    exchange(0, 2)
    own(1)
    exchange(0, 3)
    turn_values()
    near(0)
    own(2)
    exchange(1, 0)
    exchange(1, 1)
    near(1)
    own(3)
    exchange(1, 2)
    exchange(1, 3)
    distant(0)
    relayed(0)
    qc.wait()
    dense_weigh(0)
    near(2)
    distant(1)
    for g in range(4):
        exchange(2, g)
    own(4)
    make_table()
    relayed(1)
    near(3)
    own(5)
    dense_weigh(1)
    distant(2)
    relayed(2)
    near(4)
    own(6)
    dense_weigh(2)
    distant(3)
    relayed(3)
    dense_weigh(3)
    lax.fori_loop(0, 3, weigh, 0)
    own(7)
    near(5)
    distant(4)
    relayed(4)
    dense_value(0, 0)
    lax.fori_loop(3, 6, weigh, 0)
    near(6)
    distant(5)
    relayed(5)
    dense_value(0, 1)
    lax.fori_loop(6, 9, weigh, 0)
    near(7)
    own(8)
    distant(6)
    relayed(6)
    dense_value(0, 2)
    lax.fori_loop(9, 12, weigh, 0)
    distant(7)
    own(9)
    lax.fori_loop(12, 16, weigh, 0)
    relayed(7)
    near(8)
    own(10)
    dense_value(0, 3)
    value(0)
    first.stage(0)
    near(9)
    distant(8)
    own(11)
    near(10)
    distant(9)
    first.stage(1)
    near(11)
    distant(10)
    first.stage(2)
    distant(11)
    first.stage(3)
    for g in range(4):
        relayed(8 + g)
        dense_value(1, g)
    first.stage(4)
    value(1)
    second.stage(0)
    for a in both:
        unpack(a, 0, 0, None)
    second.stage(1)
    for a in both:
        unpack(a, -1, 0, None)
        unpack(a, 1, 0, None)
    first.stage(5)
    second.stage(2)
    for a in both:
        unpack(a, 0, -1, None)
        unpack(a, 0, 1, None)
    first.stage(6)
    second.stage(3)
    for a in both:
        unpack(a, 2, 0, None)
    second.stage(4)
    for a in both:
        for u in (-1, 1):
            unpack(a, u, -1, None)
            unpack(a, u, 1, None)
    second.stage(5)
    for a in both:
        unpack(a, 2, -1, None)
        unpack(a, 2, 1, None)
    for u in (0, -1, 1, 2):
        second.arrived(u, 2)
        for a in both:
            unpack(a, u, 2, None)
    for s, ref in (
        (sem.at[4], mb.at[pl.ds(0, NKA - 1)]),
        (sem.at[5], kb.at[pl.ds(0, NKA - 1)]),
        (sem.at[6], vb0.at[pl.ds(0, NKA - 1)]),
        (sem.at[7], vb1.at[pl.ds(0, NKA - 1)]),
        (z_send.at[0], kb.at[pl.ds(0, 112)]),
        (z_send.at[1], vb0.at[pl.ds(0, 112)]),
        (z_send.at[2], vb1.at[pl.ds(0, 112)]),
        (s_send.at[0], got.at[0, pl.ds(0, NKA - 1)]),
        (s_send.at[1], got.at[1, pl.ds(0, NKA - 1)]),
    ):
        remote(ref, ref, s, s, pb, ka).wait_send()


def attend(queries, keys, values, mask_t):
    any_spec = pl.BlockSpec(memory_space=pltpu.HBM)
    dma = pltpu.SemaphoreType.DMA
    vmem = pltpu.VMEM
    return pl.pallas_call(
        attend_kernel,
        out_shape=pltpu.VMEM((ROWS, HEADS * HEAD_DIM), BF16),
        in_specs=[any_spec] * 4,
        out_specs=pl.BlockSpec(memory_space=pltpu.VMEM),
        scratch_shapes=[
            vmem((2, NKA, PACKED, 128), BF16),
            vmem((ROWS, HEAD_DIM), BF16),
            vmem((BLOCK, HEADS * HEAD_DIM), BF16),
            vmem((HEADS * HEAD_DIM, BLOCK), BF16),
            vmem((NB, BLOCK, HEAD_DIM), BF16),
            vmem((NB, WAVE, BLOCK), BF16),
            vmem((NB, WAVE, BLOCK), BF16),
            vmem((NKA, 8, 128), jnp.int32),
            vmem((16, 128), jnp.int32),
            pltpu.SMEM((16, 128), jnp.int32),
            vmem((QBLOCKS, SLOTS, BLOCK, BLOCK), BF16),
            vmem((QBLOCKS, 8, 128), F32),
            vmem((NPB, 4 * BLOCK, DENSE), F32),
            vmem((4, NPB, 4 * BLOCK, DENSE), BF16),
            vmem((4, 8, DENSE), F32),
            vmem((8, DENSE), F32),
            vmem((2, WAVE, DENSE), F32),
            dma((8,)), dma((12,)), dma((3,)), dma((36,)), dma((2,)), dma((2, 10)),
        ],
        compiler_params=pltpu.CompilerParams(
            collective_id=0, has_side_effects=True, vmem_limit_bytes=58_400_000
        ),
        name="attend",
    )(queries, keys, values, mask_t)


def local(queries, keys, values, block_mask):
    mask_t = jnp.pad(block_mask.T, ((0, 0), (0, 112)))
    return attend(queries, keys, values, mask_t)


def solution(mesh):
    return jax.shard_map(
        local,
        mesh=mesh,
        in_specs=(P("pb", None), P(("ka", "pb"), None), P(("ka", "pb"), None), P("pb", "ka")),
        out_specs=P("pb", None),
        check_vma=False,
    )
```
